32 devices in a mesh: seq: 2 (over x), tok: 16 (over z, y, core).
Axes of the slice: x: 2, y: 2, z: 4, core: 2. Of those that a mesh axis runs over, the one named last changes fastest.
Arguments:
- queries: bfloat16 [8192, 4096], P(('seq', 'tok')), parts along dimension 0, may hold values from -6 to 6
- keys: bfloat16 [8192, 4096], P(('seq', 'tok')), parts along dimension 0, may hold values from -6 to 6
- values: bfloat16 [8192, 4096], P(('seq', 'tok')), parts along dimension 0, may hold values from -6 to 6
- segments: int32 [8192], P(('seq', 'tok')), parts along dimension 0, may hold values from 0 to 31, never falling along the last dimension, each value on 1 to 256 neighbouring positions
- short_filters: bfloat16 [3, 3, 4096], replicated, may hold values from -3.5 to 3.5
- mr_filter: bfloat16 [128, 256], replicated, may hold values from -0.5 to 0.5
- mr_bias: bfloat16 [4096], replicated, may hold values from -1 to 1
Outputs:
- mixed: bfloat16 [8192, 4096], P(('seq', 'tok')), parts along dimension 0
The draws below stay inside these ranges and needn't reach their ends.
There are 2 independent parts, one for each index of `seq`. The reference program is written for one: setup_inputs(seed, part) draws one part's arguments, and reference() takes and returns one part's arrays. A program takes and returns all parts, laid end to end along the dimension named above; an argument that names none is the same for every part. Nothing has to cross between parts.
Inputs may be any that keep to these rules, and one draw needn't show every extreme that they name: `segments`: document numbers never fall along the window; each document spans 1 to 256 positions, and one spans exactly 256.
All inputs are finite; a program needn't handle non-finite values.
Results may differ from the reference program's by a relative error of at most 0.0049.
Values may be sent and summed in bfloat16 or wider, within the bound.
A program may use at most 128 MiB of HBM per device.

```python
import math
import jax
import jax.numpy as jnp
import numpy as np
from jax import lax

D = 4096
GROUPS = 256
SHORT = 3
LONG = 128
TOK_DEV = 256
LENGTH = 4096
N_TOK = 16


def levels(own_key, dims, split, least, high):
    gain = 1.0
    for axis_at, blocks in split:
        draws = jax.random.uniform(jax.random.fold_in(jax.random.fold_in(own_key, 6), axis_at), (blocks,), jnp.float32, least / len(split), high / len(split))
        gain = gain * jnp.repeat(jnp.exp(draws), dims[axis_at] // blocks).reshape((-1,) + (1,) * (len(dims) - 1 - axis_at))
    return gain


def profile(amount, total, reach, skew):
    loads = [(1 << 20) // math.isqrt(grade ** skew) + 1 for grade in range(2, amount + 1)]
    rest, counts = total - reach - (amount - 1), [1] * (amount - 1)
    while rest > 0:
        candidates = [i for i in range(amount - 1) if counts[i] < reach]
        pool, left = sum([loads[i] for i in candidates]), rest
        for i in candidates:
            more = min(reach - counts[i], max(1, left * loads[i] // pool), rest)
            counts[i] = counts[i] + more
            rest = rest - more
    return np.array([reach] + counts)


def ragged_sizes(stream_key, number_of, total, reach, lean):
    if number_of == 2:
        one = jax.random.randint(stream_key, (), max(1, total - reach), min(reach, total - 1) + 1)
        return jnp.stack([one, total - one])
    sizes = jnp.asarray(profile(number_of, total, reach, lean), jnp.int32)
    twos = (number_of - 1) // 2
    donor, taker = sizes[1:1 + 2 * twos:2], sizes[2:2 + 2 * twos:2]
    slack = jnp.minimum(donor - 1, reach - taker)
    shifted = jax.random.randint(jax.random.fold_in(stream_key, 1), (twos,), 0, 1 << 20) % (slack + 1)
    sizes = sizes.at[1:1 + 2 * twos:2].set(donor - shifted).at[2:2 + 2 * twos:2].set(taker + shifted)
    return sizes[jax.random.permutation(jax.random.fold_in(stream_key, 2), number_of)]


def scatter_about(own_key, shape, spread, limit, pieces=(), kind=jnp.bfloat16):
    entries = spread * jax.random.normal(own_key, shape, jnp.float32)
    if pieces:
        entries = entries * levels(own_key, shape, pieces, -0.22, 0.18)
    return jnp.clip(entries, -limit, limit).astype(kind)


def setup_inputs(seed: int = 0, part: int = 0) -> dict:
    arg_keys = jax.random.split(jax.random.key(seed), 8)
    part_splits = jax.random.split(jax.random.fold_in(arg_keys[7], part), 8)
    return {
        "queries": scatter_about(part_splits[0], (LENGTH, D), 1.0, 6.0, ((0, 16),)),
        "keys": scatter_about(part_splits[1], (LENGTH, D), 1.0, 6.0, ((0, 16),)),
        "values": scatter_about(part_splits[2], (LENGTH, D), 1.0, 6.0, ((0, 16),)),
        "segments": jnp.searchsorted(jnp.cumsum(ragged_sizes(part_splits[3], 2 * N_TOK, LENGTH, TOK_DEV, 2)), jnp.arange(LENGTH), side="right").astype(jnp.int32),
        "short_filters": scatter_about(arg_keys[4], (3, SHORT, D), SHORT ** -0.5, 3.5),
        "mr_filter": scatter_about(arg_keys[5], (LONG, GROUPS), LONG ** -0.5, 0.5),
        "mr_bias": jnp.clip(jax.random.uniform(arg_keys[6], (D,), jnp.float32, -1.0, 1.0), -1.0, 1.0).astype(jnp.bfloat16),
    }


def short_mix(extended, marks, taps, count):
    width = taps.shape[0]
    anchor = marks[width - 1:width - 1 + count]
    total = jnp.zeros((count, extended.shape[1]), jnp.float32)
    for offset in range(width):
        begin = width - 1 - offset
        same = (marks[begin:begin + count] == anchor).astype(jnp.float32)
        total = total + taps[offset].astype(jnp.float32)[None, :] * extended[begin:begin + count].astype(jnp.float32) * same[:, None]
    return total


def long_mix(extended, marks, filters, bias, count):
    block = filters.shape[0]
    groups = filters.shape[1]
    width = extended.shape[1]
    members = width // groups
    blocks = count // block
    earlier = extended[:count].reshape(blocks, block, width)
    current = extended[block:].reshape(blocks, block, width)
    windows = jnp.concatenate([earlier, current], 1).reshape(blocks, 2 * block, groups, members)
    mark_cols = jnp.concatenate([marks[:count].reshape(blocks, block), marks[block:].reshape(blocks, block)], 1)
    mark_rows = marks[block:].reshape(blocks, block)
    row_index = jnp.arange(block)[:, None]
    col_index = jnp.arange(2 * block)[None, :]
    offset = row_index + block - col_index
    valid = (offset >= 0) & (offset < block)
    table = filters.astype(jnp.float32)[jnp.clip(offset, 0, block - 1)]
    table = jnp.where(valid[:, :, None], table, jnp.zeros((), jnp.float32))
    table = jnp.transpose(table, (2, 0, 1))

    def one_block(items):
        window, mark_col, mark_row = items
        same = (mark_col[None, :] == mark_row[:, None]).astype(jnp.float32)
        matrix = table * same[None]
        result = jnp.einsum('gij,jgc->igc', matrix, window.astype(jnp.float32))
        return result.reshape(block, width)

    result = lax.map(one_block, (windows, mark_cols, mark_rows)).reshape(count, width)
    return result + bias.astype(jnp.float32)[None, :] * extended[block:].astype(jnp.float32)


def reference(queries, keys, values, segments, short_filters, mr_filter, mr_bias):
    count = queries.shape[0]
    width = queries.shape[1]
    front = jnp.zeros((SHORT - 1, width), jnp.bfloat16)
    marks_short = jnp.concatenate([jnp.full((SHORT - 1,), -1, jnp.int32), segments.astype(jnp.int32)])
    feat_q = short_mix(jnp.concatenate([front, queries]), marks_short, short_filters[0], count)
    feat_k = short_mix(jnp.concatenate([front, keys]), marks_short, short_filters[1], count)
    feat_v = short_mix(jnp.concatenate([front, values]), marks_short, short_filters[2], count)
    product = (feat_k * feat_v).astype(jnp.bfloat16)
    extended = jnp.concatenate([jnp.zeros((LONG, width), jnp.bfloat16), product])
    marks_long = jnp.concatenate([jnp.full((LONG,), -1, jnp.int32), segments.astype(jnp.int32)])
    longer = long_mix(extended, marks_long, mr_filter, mr_bias, count)
    return (feat_q * longer).astype(jnp.bfloat16)
```

```python
import functools

import jax
import jax.numpy as jnp
from jax import lax
from jax.experimental import pallas as pl
from jax.experimental.pallas import tpu as pltpu
from jax.sharding import PartitionSpec as P

LANES = 128
TILE = 512
F32, BF16 = jnp.float32, jnp.bfloat16


def column(row, block):
    return jnp.transpose(jnp.broadcast_to(row, (block, block)))


def kernel(axis, members, tiles, q, k, v, seg_hbm, taps_hbm, filters_hbm, bias_hbm, out,
           seg, taps, filters, bias, qb, kb, vb, pt, halo, raw, edge_send, edge, seg_prev,
           hrev, comb, biasf, segc, one, two, own_head, emask, dmask, tables, gate, rest, wide,
           small_sem, raw_sem, tail_sem, head_sem, q_sem,
           send_sem, recv_sem, small_send, small_recv):
    rows, width = q.shape
    block = filters.shape[0]
    half = block // 2
    tile = width // tiles
    per = LANES // members
    keep = block - 16
    me = lax.axis_index(axis)
    size = lax.axis_size(axis)
    has_left, has_right = me > 0, me < size - 1
    left, right = jnp.maximum(me - 1, 0), jnp.minimum(me + 1, size - 1)
    barrier = pltpu.get_barrier_semaphore()

    @pl.when(has_left)
    def _():
        pl.semaphore_signal(barrier, inc=1, device_id={axis: left}, device_id_type=pl.DeviceIdType.MESH)

    def cols(c):
        return pl.ds(pl.multiple_of(c * tile, tile), tile)

    def raw_copy(i):
        return pltpu.make_async_copy((q, k, v)[i].at[pl.ds(rows - 8, 8)], raw.at[i], raw_sem.at[i])

    def tail_copy(i, c):
        at = pl.ds(keep, rows - keep)
        return pltpu.make_async_copy(
            (k, v)[i].at[at, cols(c)], (kb, vb)[i].at[c, at], tail_sem.at[i, c])

    def head_copy(i, c):
        at = pl.ds(0, keep)
        return pltpu.make_async_copy(
            (k, v)[i].at[at, cols(c)], (kb, vb)[i].at[c, at], head_sem.at[i, c])

    def q_copy(c):
        return pltpu.make_async_copy(q.at[:, cols(c)], qb.at[c], q_sem.at[c])

    def remote(src, dst, s, r):
        return pltpu.make_async_remote_copy(
            src_ref=src, dst_ref=dst, send_sem=s, recv_sem=r,
            device_id={axis: right}, device_id_type=pl.DeviceIdType.MESH)

    def product_copy(c):
        return remote(pt.at[c], halo.at[c], send_sem.at[c], recv_sem.at[c])

    def edge_copy():
        return remote(edge_send, edge, small_send.at[0], small_recv.at[0])

    def seg_copy():
        return remote(seg, seg_prev, small_send.at[1], small_recv.at[1])

    small = [
        pltpu.make_async_copy(src, dst, small_sem.at[i])
        for i, (src, dst) in enumerate(
            ((seg_hbm, seg), (taps_hbm, taps), (filters_hbm, filters), (bias_hbm, bias)))
    ]
    small[0].start()
    for i in range(3):
        raw_copy(i).start()
    small[1].start()

    @pl.loop(0, tiles)
    def _(c):
        tail_copy(0, c).start()
        tail_copy(1, c).start()

    small[2].start()
    small[3].start()

    @pl.loop(0, tiles)
    def _(c):
        head_copy(0, c).start()
        head_copy(1, c).start()
        q_copy(c).start()

    tap = lax.broadcasted_iota(jnp.int32, (half, LANES), 0)
    lane = lax.broadcasted_iota(jnp.int32, (half, LANES), 1)
    strip = lax.broadcasted_iota(jnp.int32, (16, LANES), 1) // members
    pick2 = [(strip % 2 == i).astype(BF16) for i in range(2)]
    pick4 = [(strip % 4 == i).astype(BF16) for i in range(4)]

    def short_masks(at, count):
        here = segc[pl.ds(at + block, count)]
        one[pl.ds(at, count)] = jnp.where(here == segc[pl.ds(at + block - 1, count)], 1.0, 0.0)
        two[pl.ds(at, count)] = jnp.where(here == segc[pl.ds(at + block - 2, count)], 1.0, 0.0)

    def feature(buf, x, lead, taps_rows, at, count):
        buf[pl.ds(lead, x.shape[0])] = x
        first = lead + x.shape[0] - count
        x0 = x[x.shape[0] - count:]
        x1, x2 = buf[pl.ds(first - 1, count)], buf[pl.ds(first - 2, count)]
        return (taps_rows[0:1] * x0 + (taps_rows[1:2] * x1) * one[pl.ds(at, count)]
                + (taps_rows[2:3] * x2) * two[pl.ds(at, count)])

    small[0].wait()
    for b in range(2):
        segc[pl.ds((b + 1) * block, block)] = column(seg[b:b + 1].astype(F32), block)
    short_masks(block, block)
    for i in range(3):
        raw_copy(i).wait()
    edge_send[...] = jnp.concatenate(
        [raw[i].astype(F32)[6:8] for i in range(3)] + [jnp.zeros((2, width), F32)]).astype(BF16)

    @pl.when(has_right)
    def _():
        pl.semaphore_wait(barrier, 1)
        seg_copy().start()
        edge_copy().start()

    def part(c, s):
        return pl.ds(pl.multiple_of(c * tile + s, LANES), LANES)

    def taps_of(i, at):
        return taps[i, :, at].astype(F32)

    small[1].wait()

    @pl.loop(0, tiles)
    def _(c):
        tail_copy(0, c).wait()
        tail_copy(1, c).wait()
        for s in range(0, tile, LANES):
            at, here = part(c, s), slice(s, s + LANES)
            feats = []
            for i, buf in ((1, kb), (2, vb)):
                x = buf[c, keep:, here].astype(F32)
                feats.append(feature(wide.at[i, s // LANES], x, 8, taps_of(i, at), block, block))
            pt[c, :, here] = (feats[0] * feats[1]).astype(BF16)

        @pl.when(has_right)
        def _():
            product_copy(c).start()

    small[2].wait()
    small[3].wait()
    wide_tap = lax.broadcasted_iota(jnp.int32, (block, block), 0)
    wide_lane = lax.broadcasted_iota(jnp.int32, (block, block), 1)
    turn = (wide_tap == lax.rem(block - wide_lane, block)).astype(BF16)
    turned = lax.dot_general(
        filters[...], turn, (((0,), (0,)), ((), ())), preferred_element_type=F32)
    hrev[...] = turned
    groups = turned.shape[0]
    glane = lax.broadcasted_iota(jnp.int32, turned.shape, 1)
    comb[...] = jnp.where((glane >= 1) & (glane <= half),
                          pltpu.roll(pltpu.roll(turned, half, 1), groups - 1, 0), turned)
    biasf[...] = bias[...].astype(F32)

    for b in range(4):
        own = segc[pl.ds(block + b * half, half)]
        start = own[0:1]
        own_head[pl.ds(b * half, half)] = jnp.where(own == start, 1.0, 0.0)
        row = seg[b // 2:b // 2 + 1].astype(F32)
        twin = pltpu.roll(jnp.broadcast_to(row, (8, block)), half, 1)[0:1]
        low = lane[0:1] < half
        row = jnp.where(low, row, twin) if b % 2 == 0 else jnp.where(low, twin, row)
        inner = jnp.where(lane < half, lane, lane - half)
        dmask[b] = jnp.where((own == row) & (inner <= tap), 1.0, 0.0).astype(BF16)

    def early_masks(b):
        start = segc[pl.ds(block + b * half, 8)][0:1]
        same = jnp.where(segc[pl.ds(b * half, block)] == start, 1.0, 0.0).astype(BF16)
        for i in range(2):
            emask[b, i] = same * jnp.concatenate([pick2[i]] * (block // 16), 0)

    early_masks(2)
    early_masks(3)
    later = (lane > tap).astype(BF16)

    @pl.when(has_left)
    def _():
        seg_copy().wait_recv()
        edge_copy().wait_recv()

    @pl.when(jnp.logical_not(has_left))
    def _():
        seg_prev[...] = jnp.zeros_like(seg_prev)
        edge[...] = jnp.zeros_like(edge)

        @pl.loop(0, tiles)
        def _(c):
            halo[c] = jnp.zeros_like(halo[c])

    segc[pl.ds(0, block)] = column(seg_prev[1:2].astype(F32), block)
    short_masks(0, block)
    early_masks(0)
    early_masks(1)

    quad = lax.broadcasted_iota(jnp.int32, (half, LANES), 1) // (2 * members)

    def early(table, low, high, b):
        right_side = jnp.concatenate([
            jnp.concatenate([x * emask[b + j, i] for j, x in enumerate((low, high))], 1)
            for i in range(2)], 0)
        every = jnp.dot(table, right_side, preferred_element_type=F32)
        picked = []
        for j in range(2):
            side = every[:, j * LANES:(j + 1) * LANES]
            parts = [side[h * half:(h + 1) * half] for h in range(4)]
            picked.append(jnp.where(quad == 0, parts[0], jnp.where(
                quad == 1, parts[1], jnp.where(quad == 2, parts[2], parts[3]))))
        return jnp.concatenate(picked, 0)

    @pl.loop(0, tiles)
    def _(c):
        head_copy(0, c).wait()
        head_copy(1, c).wait()
        q_copy(c).wait()
        for s in range(0, tile, LANES):
            at, here, n = part(c, s), slice(s, s + LANES), s // LANES
            edges = edge[:, at].astype(F32)

            def feat(i, buf, count):
                wide[i, n, pl.ds(6, 2)] = edges[2 * i:2 * i + 2]
                return feature(wide.at[i, n], buf[c, :count, here].astype(F32), 8, taps_of(i, at), 0, count)

            mid = (feat(1, kb, block) * feat(2, vb, block)).astype(BF16)
            near = pt[c, :, here]
            first = (c * tile + s) // members

            def ring(source, g):
                base = jnp.broadcast_to(source[pl.ds(first + g, 1), :], (half, block))
                return pltpu.roll(base, 0, 1, stride=1, stride_axis=0).astype(BF16)

            for h in range(4):
                for i in range(2):
                    tables[c, n, h * half:(h + 1) * half, i * block:(i + 1) * block] = ring(hrev, 2 * h + i) * later
            own = [[ring(comb, 4 * h + 2 * i) for i in range(2)] for h in range(2)]
            blocks = (mid[:half], mid[half:], near[:half], near[half:])
            diag = []
            for b in range(4):
                left_side = jnp.concatenate([
                    jnp.concatenate([own[h][i] * dmask[b] for i in range(2)], 1) for h in range(2)], 0)
                right_side = jnp.concatenate([
                    blocks[b] * jnp.concatenate([pick4[i]] * (half // 16), 0) for i in range(4)], 0)
                every = jnp.dot(left_side, right_side, preferred_element_type=F32)
                diag.append(jnp.where(quad < 2, every[:half], every[half:]))
            brow = biasf[pl.ds((c * tile + s) // LANES, 1), :]
            fq = feat(0, qb, rows)
            sure0 = jnp.concatenate(diag[:2], 0) + brow * mid.astype(F32)
            gate[c, n] = fq[:block] * own_head[pl.ds(0, block)]
            rest[c, n] = fq[:block] * sure0
            fresh = early(tables[c, n], mid, jnp.concatenate([mid[half:], near[:half]], 0), 2)
            sure1 = jnp.concatenate(diag[2:], 0) + brow * near.astype(F32)
            out[block:, at] = (fq[block:] * (sure1 + fresh * own_head[pl.ds(block, block)])).astype(BF16)
            kb[c, :half, here] = mid[:half]

    @pl.loop(0, tiles)
    def _(c):
        @pl.when(has_left)
        def _():
            product_copy(c).wait_recv()

        for s in range(0, tile, LANES):
            at, here, n = part(c, s), slice(s, s + LANES), s // LANES
            far = halo[c, :, here]
            fresh = early(tables[c, n], far, jnp.concatenate([far[half:], kb[c, :half, here]], 0), 0)
            out[:block, at] = (gate[c, n] * fresh + rest[c, n]).astype(BF16)

    @pl.when(has_right)
    def _():
        seg_copy().wait_send()
        edge_copy().wait_send()

        @pl.loop(0, tiles)
        def _(c):
            product_copy(c).wait_send()


def per_device(queries, keys, values, segments, short_filters, mr_filter, mr_bias):
    rows, width = queries.shape
    block, groups = mr_filter.shape
    half = block // 2
    members = width // groups
    tile = min(TILE, width)
    tiles = width // tile
    parts = tile // LANES
    dma = pltpu.SemaphoreType.DMA
    chunked = lambda r: pltpu.VMEM((tiles, r, tile), BF16)
    return pl.pallas_call(
        functools.partial(kernel, "tok", members, tiles),
        in_specs=[pl.BlockSpec(memory_space=pltpu.HBM)] * 7,
        out_specs=pl.BlockSpec(memory_space=pltpu.VMEM),
        out_shape=pltpu.VMEM((rows, width), BF16),
        scratch_shapes=[
            pltpu.VMEM((rows // block, block), jnp.int32),
            pltpu.VMEM(short_filters.shape, BF16),
            pltpu.VMEM(mr_filter.shape, BF16),
            pltpu.VMEM((width // LANES, LANES), BF16),
            chunked(rows), chunked(rows), chunked(rows),
            chunked(block), chunked(block),
            pltpu.VMEM((3, 8, width), BF16),
            pltpu.VMEM((8, width), BF16),
            pltpu.VMEM((8, width), BF16),
            pltpu.VMEM((rows // block, block), jnp.int32),
            pltpu.VMEM((groups, block), F32),
            pltpu.VMEM((groups, block), F32),
            pltpu.VMEM((width // LANES, LANES), F32),
            pltpu.VMEM((block + rows, LANES), F32),
            pltpu.VMEM((rows, LANES), F32),
            pltpu.VMEM((rows, LANES), F32),
            pltpu.VMEM((rows, LANES), F32),
            pltpu.VMEM((4, 2, block, LANES), BF16),
            pltpu.VMEM((4, half, LANES), BF16),
            pltpu.VMEM((tiles, parts, 4 * half, 2 * block), BF16),
            pltpu.VMEM((tiles, parts, block, LANES), F32),
            pltpu.VMEM((tiles, parts, block, LANES), F32),
            pltpu.VMEM((3, parts, rows + 8, LANES), F32),
            dma((4,)), dma((3,)), dma((2, tiles)), dma((2, tiles)), dma((tiles,)),
            dma((tiles,)), dma((tiles,)), dma((2,)), dma((2,)),
        ],
        compiler_params=pltpu.CompilerParams(
            collective_id=0, has_side_effects=True, vmem_limit_bytes=40 * 2**20
        ),
    )(*(pltpu.with_memory_space_constraint(x, pltpu.HBM) for x in (
        queries, keys, values, segments.reshape(rows // block, block), short_filters,
        mr_filter, mr_bias.reshape(width // LANES, LANES))))


def solution(mesh):
    placed = (
        P(("seq", "tok"), None),
        P(("seq", "tok"), None),
        P(("seq", "tok"), None),
        P(("seq", "tok")),
        P(),
        P(),
        P(),
    )
    return jax.shard_map(
        per_device, mesh=mesh, in_specs=placed, out_specs=P(("seq", "tok"), None), check_vma=False
    )
```

```python
import functools

import jax
import jax.numpy as jnp
from jax import lax
from jax.experimental import pallas as pl
from jax.experimental.pallas import tpu as pltpu
from jax.sharding import PartitionSpec as P

LANES = 128
TILE = 512
LAST = 2
F32, BF16 = jnp.float32, jnp.bfloat16


def column(row, block):
    return jnp.transpose(jnp.broadcast_to(row, (block, block)))


def quads(half, members):
    return lax.broadcasted_iota(jnp.int32, (half, LANES), 1) // (2 * members)


def early(table, low, high, masks, quad):
    half = quad.shape[0]
    right_side = jnp.concatenate([
        jnp.concatenate([x * masks[j, i] for j, x in enumerate((low, high))], 1)
        for i in range(2)], 0)
    every = jnp.dot(table, right_side, preferred_element_type=F32)
    picked = []
    for j in range(2):
        side = every[:, j * LANES:(j + 1) * LANES]
        parts = [side[h * half:(h + 1) * half] for h in range(4)]
        picked.append(jnp.where(quad == 0, parts[0], jnp.where(
            quad == 1, parts[1], jnp.where(quad == 2, parts[2], parts[3]))))
    return jnp.concatenate(picked, 0)


def join(c, n, here, halo, mids, tables, gate, rest, masks, quad):
    half = quad.shape[0]
    far = halo[c, :, here]
    fresh = early(tables[c, n], far, jnp.concatenate([far[half:], mids[c, :, here]], 0), masks, quad)
    return (gate[c, n] * fresh + rest[c, n]).astype(BF16)


def kernel(axis, members, tiles, last, q, k, v, seg_hbm, taps_hbm, filters_hbm, bias_hbm,
           out, halo, mids, tables, gate, rest, emask,
           seg, taps, filters, bias, qb, kv, pt, raw, edge_send, edge, seg_prev,
           hrev, comb, biasf, segc, one, two, own_head, dmask, wide,
           small_sem, raw_sem, tail_sem, head_sem, q_sem,
           send_sem, recv_sem, small_send, small_recv):
    rows, width = q.shape
    block = filters.shape[0]
    half = block // 2
    tile = width // tiles
    per = LANES // members
    keep = block - 16
    me = lax.axis_index(axis)
    size = lax.axis_size(axis)
    has_left, has_right = me > 0, me < size - 1
    left, right = jnp.maximum(me - 1, 0), jnp.minimum(me + 1, size - 1)
    barrier = pltpu.get_barrier_semaphore()

    @pl.when(has_left)
    def _():
        pl.semaphore_signal(barrier, inc=1, device_id={axis: left}, device_id_type=pl.DeviceIdType.MESH)

    def cols(c):
        return pl.ds(pl.multiple_of(c * tile, tile), tile)

    def raw_copy(i):
        return pltpu.make_async_copy((q, k, v)[i].at[pl.ds(rows - 8, 8)], raw.at[i], raw_sem.at[0])

    def tail_copy(i, c):
        at = pl.ds(keep, rows - keep)
        return pltpu.make_async_copy((k, v)[i].at[at, cols(c)], kv.at[i, c, at], tail_sem.at[c])

    def head_copy(i, c):
        at = pl.ds(0, keep)
        return pltpu.make_async_copy((k, v)[i].at[at, cols(c)], kv.at[i, c, at], head_sem.at[c])

    def whole(ref, sem):
        return pltpu.make_async_copy(ref, ref, sem)

    def q_copy(c):
        return pltpu.make_async_copy(q.at[:, cols(c)], qb.at[c], q_sem.at[c])

    def remote(src, dst, s, r):
        return pltpu.make_async_remote_copy(
            src_ref=src, dst_ref=dst, send_sem=s, recv_sem=r,
            device_id={axis: right}, device_id_type=pl.DeviceIdType.MESH)

    def product_copy(c):
        return remote(pt.at[c], halo.at[c], send_sem.at[0], recv_sem.at[c])

    def edge_copy():
        return remote(edge_send, edge, small_send.at[0], small_recv.at[0])

    def seg_copy():
        return remote(seg, seg_prev, small_send.at[1], small_recv.at[1])

    small = [
        pltpu.make_async_copy(src, dst, small_sem.at[i])
        for i, (src, dst) in enumerate(
            ((seg_hbm, seg), (taps_hbm, taps), (filters_hbm, filters), (bias_hbm, bias)))
    ]
    small[0].start()
    for i in range(3):
        raw_copy(i).start()
    small[1].start()

    @pl.loop(0, tiles)
    def _(c):
        tail_copy(0, c).start()
        tail_copy(1, c).start()

    small[2].start()
    small[3].start()

    @pl.loop(0, tiles)
    def _(c):
        head_copy(0, c).start()
        head_copy(1, c).start()
        q_copy(c).start()

    tap = lax.broadcasted_iota(jnp.int32, (half, LANES), 0)
    lane = lax.broadcasted_iota(jnp.int32, (half, LANES), 1)
    strip = lax.broadcasted_iota(jnp.int32, (16, LANES), 1) // members
    pick2 = [(strip % 2 == i).astype(BF16) for i in range(2)]
    pick4 = [(strip % 4 == i).astype(BF16) for i in range(4)]

    def short_masks(at, count):
        here = segc[pl.ds(at + block, count)]
        one[pl.ds(at, count)] = jnp.where(here == segc[pl.ds(at + block - 1, count)], 1.0, 0.0)
        two[pl.ds(at, count)] = jnp.where(here == segc[pl.ds(at + block - 2, count)], 1.0, 0.0)

    def feature(buf, x, lead, taps_rows, at, count):
        buf[pl.ds(lead, x.shape[0])] = x
        first = lead + x.shape[0] - count
        x0 = x[x.shape[0] - count:]
        x1, x2 = buf[pl.ds(first - 1, count)], buf[pl.ds(first - 2, count)]
        return (taps_rows[0:1] * x0 + (taps_rows[1:2] * x1) * one[pl.ds(at, count)]
                + (taps_rows[2:3] * x2) * two[pl.ds(at, count)])

    small[0].wait()
    for b in range(2):
        segc[pl.ds((b + 1) * block, block)] = column(seg[b:b + 1].astype(F32), block)
    short_masks(block, block)
    whole(raw, raw_sem.at[0]).wait()
    for i in range(3):
        edge_send[i] = raw[i].astype(F32)[6:8].astype(BF16)

    def part(c, s):
        return pl.ds(pl.multiple_of(c * tile + s, LANES), LANES)

    def taps_of(i, at):
        return taps[i, :, at].astype(F32)

    small[1].wait()

    @pl.loop(0, tiles)
    def _(c):
        whole(kv.at[:, c, pl.ds(keep, rows - keep)], tail_sem.at[c]).wait()
        for s in range(0, tile, LANES):
            at, here = part(c, s), slice(s, s + LANES)
            feats = []
            for i in (1, 2):
                x = kv[i - 1, c, keep:, here].astype(F32)
                feats.append(feature(wide.at[i, s // LANES], x, 8, taps_of(i, at), block, block))
            pt[c, :, here] = (feats[0] * feats[1]).astype(BF16)

        @pl.when(has_right & (c == 0))
        def _():
            pl.semaphore_wait(barrier, 1)
            seg_copy().start()
            edge_copy().start()

        @pl.when(has_right)
        def _():
            product_copy(c).start()

    small[2].wait()
    small[3].wait()
    wide_tap = lax.broadcasted_iota(jnp.int32, (block, block), 0)
    wide_lane = lax.broadcasted_iota(jnp.int32, (block, block), 1)
    turn = (wide_tap == lax.rem(block - wide_lane, block)).astype(BF16)
    turned = lax.dot_general(
        filters[...], turn, (((0,), (0,)), ((), ())), preferred_element_type=F32)
    hrev[...] = turned
    groups = turned.shape[0]
    glane = lax.broadcasted_iota(jnp.int32, turned.shape, 1)
    comb[...] = jnp.where((glane >= 1) & (glane <= half),
                          pltpu.roll(pltpu.roll(turned, half, 1), groups - 1, 0), turned)
    biasf[...] = bias[...].astype(F32)

    for b in range(4):
        own = segc[pl.ds(block + b * half, half)]
        start = own[0:1]
        own_head[pl.ds(b * half, half)] = jnp.where(own == start, 1.0, 0.0)
        row = seg[b // 2:b // 2 + 1].astype(F32)
        twin = pltpu.roll(jnp.broadcast_to(row, (8, block)), half, 1)[0:1]
        low = lane[0:1] < half
        row = jnp.where(low, row, twin) if b % 2 == 0 else jnp.where(low, twin, row)
        inner = jnp.where(lane < half, lane, lane - half)
        dmask[b] = jnp.where((own == row) & (inner <= tap), 1.0, 0.0).astype(BF16)

    def early_masks(b):
        start = segc[pl.ds(block + b * half, 8)][0:1]
        same = jnp.where(segc[pl.ds(b * half, block)] == start, 1.0, 0.0).astype(BF16)
        for i in range(2):
            emask[b, i] = same * jnp.concatenate([pick2[i]] * (block // 16), 0)

    early_masks(2)
    early_masks(3)
    later = (lane > tap).astype(BF16)

    @pl.when(has_left)
    def _():
        seg_copy().wait_recv()
        edge_copy().wait_recv()

    @pl.when(jnp.logical_not(has_left))
    def _():
        seg_prev[...] = jnp.zeros_like(seg_prev)
        edge[...] = jnp.zeros_like(edge)

        @pl.loop(0, tiles)
        def _(c):
            halo[c] = jnp.zeros_like(halo[c])

    segc[pl.ds(0, block)] = column(seg_prev[1:2].astype(F32), block)
    short_masks(0, block)
    early_masks(0)
    early_masks(1)

    quad = quads(half, members)

    @pl.loop(0, tiles)
    def _(c):
        whole(kv.at[:, c, pl.ds(0, keep)], head_sem.at[c]).wait()
        q_copy(c).wait()
        for s in range(0, tile, LANES):
            at, here, n = part(c, s), slice(s, s + LANES), s // LANES

            def feat(i, x):
                wide[i, n, pl.ds(6, 2)] = edge[i, :, at].astype(F32)
                return feature(wide.at[i, n], x.astype(F32), 8, taps_of(i, at), 0, x.shape[0])

            mid = (feat(1, kv[0, c, :block, here]) * feat(2, kv[1, c, :block, here])).astype(BF16)
            near = pt[c, :, here]
            first = (c * tile + s) // members

            def ring(source, g):
                base = jnp.broadcast_to(source[pl.ds(first + g, 1), :], (half, block))
                return pltpu.roll(base, 0, 1, stride=1, stride_axis=0).astype(BF16)

            for h in range(4):
                for i in range(2):
                    tables[c, n, h * half:(h + 1) * half, i * block:(i + 1) * block] = ring(hrev, 2 * h + i) * later
            own = [[ring(comb, 4 * h + 2 * i) for i in range(2)] for h in range(2)]
            blocks = (mid[:half], mid[half:], near[:half], near[half:])
            diag = []
            for b in range(4):
                left_side = jnp.concatenate([
                    jnp.concatenate([own[h][i] * dmask[b] for i in range(2)], 1) for h in range(2)], 0)
                right_side = jnp.concatenate([
                    blocks[b] * jnp.concatenate([pick4[i]] * (half // 16), 0) for i in range(4)], 0)
                every = jnp.dot(left_side, right_side, preferred_element_type=F32)
                diag.append(jnp.where(quad < 2, every[:half], every[half:]))
            brow = biasf[pl.ds((c * tile + s) // LANES, 1), :]
            fq = feat(0, qb[c, :, here])
            sure0 = jnp.concatenate(diag[:2], 0) + brow * mid.astype(F32)
            gate[c, n] = fq[:block] * own_head[pl.ds(0, block)]
            rest[c, n] = fq[:block] * sure0
            fresh = early(tables[c, n], mid, jnp.concatenate([mid[half:], near[:half]], 0), emask.at[2:4], quad)
            sure1 = jnp.concatenate(diag[2:], 0) + brow * near.astype(F32)
            out[block:, at] = (fq[block:] * (sure1 + fresh * own_head[pl.ds(block, block)])).astype(BF16)
            mids[c, :, here] = mid[:half]

    def arrive(c):
        @pl.when(has_left)
        def _():
            product_copy(c).wait_recv()

    @pl.loop(0, tiles - last)
    def _(c):
        arrive(c)
        for s in range(0, tile, LANES):
            out[:block, part(c, s)] = join(
                c, s // LANES, slice(s, s + LANES), halo, mids, tables, gate, rest, emask.at[0:2], quad)

    @pl.loop(tiles - last, tiles)
    def _(c):
        arrive(c)

    @pl.when(has_right)
    def _():
        seg_copy().wait_send()
        edge_copy().wait_send()
        remote(pt, halo, send_sem.at[0], recv_sem.at[0]).wait_send()


def finish(last, members, done, halo, mids, tables, gate, rest, emask, out, fresh, sem):
    rows, width = done.shape
    tiles, block, tile = halo.shape
    half = mids.shape[1]
    quad = quads(half, members)
    ready = width - last * tile
    copies = [
        pltpu.make_async_copy(done.at[at], out.at[at], sem.at[i])
        for i, at in enumerate((
            (pl.ds(0, block), pl.ds(0, ready)),
            (pl.ds(block, half), slice(None)),
            (pl.ds(block + half, half), slice(None))))]
    for copy in copies:
        copy.start()
    for i in range(last):
        c = tiles - last + i
        for s in range(0, tile, LANES):
            here = slice(s, s + LANES)
            fresh[i, :, here] = join(c, s // LANES, here, halo, mids, tables, gate, rest, emask.at[0:2], quad)
        copy = pltpu.make_async_copy(
            fresh.at[i], out.at[pl.ds(0, block), pl.ds(ready + i * tile, tile)], sem.at[3 + i])
        copy.start()
        copies.append(copy)
    for copy in copies:
        copy.wait()


def per_device(queries, keys, values, segments, short_filters, mr_filter, mr_bias):
    rows, width = queries.shape
    block, groups = mr_filter.shape
    half = block // 2
    members = width // groups
    tile = min(TILE, width)
    tiles = width // tile
    parts = tile // LANES
    dma = pltpu.SemaphoreType.DMA
    chunked = lambda r: pltpu.VMEM((tiles, r, tile), BF16)
    last = min(LAST, tiles)
    vmem = pl.BlockSpec(memory_space=pltpu.VMEM)
    held = pl.pallas_call(
        functools.partial(kernel, "tok", members, tiles, last),
        in_specs=[pl.BlockSpec(memory_space=pltpu.HBM)] * 7,
        out_specs=[vmem] * 7,
        out_shape=[
            pltpu.VMEM((rows, width), BF16),
            chunked(block),
            chunked(half),
            pltpu.VMEM((tiles, parts, 4 * half, 2 * block), BF16),
            pltpu.VMEM((tiles, parts, block, LANES), F32),
            pltpu.VMEM((tiles, parts, block, LANES), F32),
            pltpu.VMEM((4, 2, block, LANES), BF16),
        ],
        scratch_shapes=[
            pltpu.VMEM((rows // block, block), jnp.int32),
            pltpu.VMEM(short_filters.shape, BF16),
            pltpu.VMEM(mr_filter.shape, BF16),
            pltpu.VMEM((width // LANES, LANES), BF16),
            chunked(rows),
            pltpu.VMEM((2, tiles, rows, tile), BF16),
            chunked(block),
            pltpu.VMEM((3, 8, width), BF16),
            pltpu.VMEM((3, 2, width), BF16),
            pltpu.VMEM((3, 2, width), BF16),
            pltpu.VMEM((rows // block, block), jnp.int32),
            pltpu.VMEM((groups, block), F32),
            pltpu.VMEM((groups, block), F32),
            pltpu.VMEM((width // LANES, LANES), F32),
            pltpu.VMEM((block + rows, LANES), F32),
            pltpu.VMEM((rows, LANES), F32),
            pltpu.VMEM((rows, LANES), F32),
            pltpu.VMEM((rows, LANES), F32),
            pltpu.VMEM((4, half, LANES), BF16),
            pltpu.VMEM((3, parts, rows + 8, LANES), F32),
            dma((4,)), dma((1,)), dma((tiles,)), dma((tiles,)), dma((tiles,)),
            dma((1,)), dma((tiles,)), dma((2,)), dma((2,)),
        ],
        compiler_params=pltpu.CompilerParams(
            collective_id=0, has_side_effects=True, vmem_limit_bytes=24 * 2**20
        ),
    )(*(pltpu.with_memory_space_constraint(x, pltpu.HBM) for x in (
        queries, keys, values, segments.reshape(rows // block, block), short_filters,
        mr_filter, mr_bias.reshape(width // LANES, LANES))))
    return pl.pallas_call(
        functools.partial(finish, last, members),
        in_specs=[vmem] * 7,
        out_specs=pl.BlockSpec(memory_space=pltpu.HBM),
        out_shape=pltpu.HBM((rows, width), BF16),
        scratch_shapes=[pltpu.VMEM((last, block, tile), BF16), dma((3 + last,))],
        compiler_params=pltpu.CompilerParams(vmem_limit_bytes=8 * 2**20),
    )(*(pltpu.with_memory_space_constraint(x, pltpu.VMEM) for x in held))


def solution(mesh):
    placed = (
        P(("seq", "tok"), None),
        P(("seq", "tok"), None),
        P(("seq", "tok"), None),
        P(("seq", "tok")),
        P(),
        P(),
        P(),
    )
    return jax.shard_map(
        per_device, mesh=mesh, in_specs=placed, out_specs=P(("seq", "tok"), None), check_vma=False
    )
```

```python
import functools

import jax
import jax.numpy as jnp
from jax import lax
from jax.experimental import pallas as pl
from jax.experimental.pallas import tpu as pltpu
from jax.sharding import PartitionSpec as P

LANES = 128
TILE = 512
LAST = 3
F32, BF16 = jnp.float32, jnp.bfloat16


def column(row, block):
    return jnp.transpose(jnp.broadcast_to(row, (block, block)))


def quads(half, members):
    return lax.broadcasted_iota(jnp.int32, (half, LANES), 1) // (2 * members)


def early(table, low, high, masks, quad):
    half = quad.shape[0]
    right_side = jnp.concatenate([
        jnp.concatenate([x * masks[j, i] for j, x in enumerate((low, high))], 1)
        for i in range(2)], 0)
    every = jnp.dot(table, right_side, preferred_element_type=F32)
    picked = []
    for j in range(2):
        side = every[:, j * LANES:(j + 1) * LANES]
        parts = [side[h * half:(h + 1) * half] for h in range(4)]
        picked.append(jnp.where(quad == 0, parts[0], jnp.where(
            quad == 1, parts[1], jnp.where(quad == 2, parts[2], parts[3]))))
    return jnp.concatenate(picked, 0)


def join(c, n, here, halo, mids, tables, gate, rest, masks, quad):
    half = quad.shape[0]
    far = halo[c, :, here]
    fresh = early(tables[c, n], far, jnp.concatenate([far[half:], mids[c, :, here]], 0), masks, quad)
    return (gate[c, n] * fresh + rest[c, n]).astype(BF16)


def kernel(axis, members, tiles, last, q, k, v, seg_hbm, taps_hbm, filters_hbm, bias_hbm,
           out, halo, mids, tables, gate, rest, emask,
           seg, taps, filters, bias, qb, kv, pt, raw, edge_send, edge, seg_prev,
           hrev, comb, biasf, segc, one, two, own_head, dmask, wide,
           small_sem, raw_sem, tail_sem, head_sem, q_sem,
           send_sem, recv_sem, small_send, small_recv):
    rows, width = q.shape
    block = filters.shape[0]
    half = block // 2
    tile = width // tiles
    per = LANES // members
    keep = block - 16
    me = lax.axis_index(axis)
    size = lax.axis_size(axis)
    has_left, has_right = me > 0, me < size - 1
    left, right = jnp.maximum(me - 1, 0), jnp.minimum(me + 1, size - 1)
    barrier = pltpu.get_barrier_semaphore()

    @pl.when(has_left)
    def _():
        pl.semaphore_signal(barrier, inc=1, device_id={axis: left}, device_id_type=pl.DeviceIdType.MESH)

    def cols(c):
        return pl.ds(pl.multiple_of(c * tile, tile), tile)

    def raw_copy(i):
        return pltpu.make_async_copy((q, k, v)[i].at[pl.ds(rows - 8, 8)], raw.at[i], raw_sem.at[0])

    def tail_copy(i, c):
        at = pl.ds(keep, rows - keep)
        return pltpu.make_async_copy((k, v)[i].at[at, cols(c)], kv.at[i, c, at], tail_sem.at[c])

    def head_copy(i, c):
        at = pl.ds(0, keep)
        return pltpu.make_async_copy((k, v)[i].at[at, cols(c)], kv.at[i, c, at], head_sem.at[c])

    def whole(ref, sem):
        return pltpu.make_async_copy(ref, ref, sem)

    def q_copy(c):
        return pltpu.make_async_copy(q.at[:, cols(c)], qb.at[c], q_sem.at[c])

    def remote(src, dst, s, r):
        return pltpu.make_async_remote_copy(
            src_ref=src, dst_ref=dst, send_sem=s, recv_sem=r,
            device_id={axis: right}, device_id_type=pl.DeviceIdType.MESH)

    def product_copy(c):
        return remote(pt.at[c], halo.at[c], send_sem.at[0], recv_sem.at[c])

    def edge_copy():
        return remote(edge_send, edge, small_send.at[0], small_recv.at[0])

    def seg_copy():
        return remote(seg, seg_prev, small_send.at[1], small_recv.at[1])

    small = [
        pltpu.make_async_copy(src, dst, small_sem.at[i])
        for i, (src, dst) in enumerate(
            ((seg_hbm, seg), (taps_hbm, taps), (filters_hbm, filters), (bias_hbm, bias)))
    ]
    small[0].start()
    for i in range(3):
        raw_copy(i).start()
    small[1].start()

    @pl.loop(0, tiles)
    def _(c):
        tail_copy(0, c).start()
        tail_copy(1, c).start()

    small[2].start()
    small[3].start()

    @pl.loop(0, tiles)
    def _(c):
        head_copy(0, c).start()
        head_copy(1, c).start()
        q_copy(c).start()

    tap = lax.broadcasted_iota(jnp.int32, (half, LANES), 0)
    lane = lax.broadcasted_iota(jnp.int32, (half, LANES), 1)
    strip = lax.broadcasted_iota(jnp.int32, (16, LANES), 1) // members
    pick2 = [(strip % 2 == i).astype(BF16) for i in range(2)]
    pick4 = [(strip % 4 == i).astype(BF16) for i in range(4)]

    def short_masks(at, count):
        here = segc[pl.ds(at + block, count)]
        one[pl.ds(at, count)] = jnp.where(here == segc[pl.ds(at + block - 1, count)], 1.0, 0.0)
        two[pl.ds(at, count)] = jnp.where(here == segc[pl.ds(at + block - 2, count)], 1.0, 0.0)

    def feature(buf, x, lead, taps_rows, at, count):
        buf[pl.ds(lead, x.shape[0])] = x
        first = lead + x.shape[0] - count
        x0 = x[x.shape[0] - count:]
        x1, x2 = buf[pl.ds(first - 1, count)], buf[pl.ds(first - 2, count)]
        return (taps_rows[0:1] * x0 + (taps_rows[1:2] * x1) * one[pl.ds(at, count)]
                + (taps_rows[2:3] * x2) * two[pl.ds(at, count)])

    small[0].wait()
    for b in range(2):
        segc[pl.ds((b + 1) * block, block)] = column(seg[b:b + 1].astype(F32), block)
    short_masks(block, block)
    whole(raw, raw_sem.at[0]).wait()
    for i in range(3):
        edge_send[i] = raw[i].astype(F32)[6:8].astype(BF16)

    def part(c, s):
        return pl.ds(pl.multiple_of(c * tile + s, LANES), LANES)

    def taps_of(i, at):
        return taps[i, :, at].astype(F32)

    small[1].wait()

    @pl.loop(0, tiles)
    def _(c):
        whole(kv.at[:, c, pl.ds(keep, rows - keep)], tail_sem.at[c]).wait()
        for s in range(0, tile, LANES):
            at, here = part(c, s), slice(s, s + LANES)
            feats = []
            for i in (1, 2):
                x = kv[i - 1, c, keep:, here].astype(F32)
                feats.append(feature(wide.at[i, s // LANES], x, 8, taps_of(i, at), block, block))
            pt[c, :, here] = (feats[0] * feats[1]).astype(BF16)

        @pl.when(has_right & (c == 0))
        def _():
            pl.semaphore_wait(barrier, 1)
            seg_copy().start()
            edge_copy().start()

        @pl.when(has_right)
        def _():
            product_copy(c).start()

    small[2].wait()
    small[3].wait()
    wide_tap = lax.broadcasted_iota(jnp.int32, (block, block), 0)
    wide_lane = lax.broadcasted_iota(jnp.int32, (block, block), 1)
    turn = (wide_tap == lax.rem(block - wide_lane, block)).astype(BF16)
    turned = lax.dot_general(
        filters[...], turn, (((0,), (0,)), ((), ())), preferred_element_type=F32)
    hrev[...] = turned
    groups = turned.shape[0]
    glane = lax.broadcasted_iota(jnp.int32, turned.shape, 1)
    comb[...] = jnp.where((glane >= 1) & (glane <= half),
                          pltpu.roll(pltpu.roll(turned, half, 1), groups - 1, 0), turned)
    biasf[...] = bias[...].astype(F32)

    for b in range(4):
        own = segc[pl.ds(block + b * half, half)]
        start = own[0:1]
        own_head[pl.ds(b * half, half)] = jnp.where(own == start, 1.0, 0.0)
        row = seg[b // 2:b // 2 + 1].astype(F32)
        twin = pltpu.roll(jnp.broadcast_to(row, (8, block)), half, 1)[0:1]
        low = lane[0:1] < half
        row = jnp.where(low, row, twin) if b % 2 == 0 else jnp.where(low, twin, row)
        inner = jnp.where(lane < half, lane, lane - half)
        dmask[b] = jnp.where((own == row) & (inner <= tap), 1.0, 0.0).astype(BF16)

    def early_masks(b):
        start = segc[pl.ds(block + b * half, 8)][0:1]
        same = jnp.where(segc[pl.ds(b * half, block)] == start, 1.0, 0.0).astype(BF16)
        for i in range(2):
            emask[b, i] = same * jnp.concatenate([pick2[i]] * (block // 16), 0)

    early_masks(2)
    early_masks(3)
    later = (lane > tap).astype(BF16)

    @pl.when(has_left)
    def _():
        seg_copy().wait_recv()
        edge_copy().wait_recv()

    @pl.when(jnp.logical_not(has_left))
    def _():
        seg_prev[...] = jnp.zeros_like(seg_prev)
        edge[...] = jnp.zeros_like(edge)

        @pl.loop(0, tiles)
        def _(c):
            halo[c] = jnp.zeros_like(halo[c])

    segc[pl.ds(0, block)] = column(seg_prev[1:2].astype(F32), block)
    short_masks(0, block)
    early_masks(0)
    early_masks(1)

    quad = quads(half, members)

    @pl.loop(0, tiles)
    def _(c):
        whole(kv.at[:, c, pl.ds(0, keep)], head_sem.at[c]).wait()
        q_copy(c).wait()
        for s in range(0, tile, LANES):
            at, here, n = part(c, s), slice(s, s + LANES), s // LANES

            def feat(i, x):
                wide[i, n, pl.ds(6, 2)] = edge[i, :, at].astype(F32)
                return feature(wide.at[i, n], x.astype(F32), 8, taps_of(i, at), 0, x.shape[0])

            mid = (feat(1, kv[0, c, :block, here]) * feat(2, kv[1, c, :block, here])).astype(BF16)
            near = pt[c, :, here]
            first = (c * tile + s) // members

            def ring(source, g):
                base = jnp.broadcast_to(source[pl.ds(first + g, 1), :], (half, block))
                return pltpu.roll(base, 0, 1, stride=1, stride_axis=0).astype(BF16)

            for h in range(4):
                for i in range(2):
                    tables[c, n, h * half:(h + 1) * half, i * block:(i + 1) * block] = ring(hrev, 2 * h + i) * later
            own = [[ring(comb, 4 * h + 2 * i) for i in range(2)] for h in range(2)]
            blocks = (mid[:half], mid[half:], near[:half], near[half:])
            diag = []
            for b in range(4):
                left_side = jnp.concatenate([
                    jnp.concatenate([own[h][i] * dmask[b] for i in range(2)], 1) for h in range(2)], 0)
                right_side = jnp.concatenate([
                    blocks[b] * jnp.concatenate([pick4[i]] * (half // 16), 0) for i in range(4)], 0)
                every = jnp.dot(left_side, right_side, preferred_element_type=F32)
                diag.append(jnp.where(quad < 2, every[:half], every[half:]))
            brow = biasf[pl.ds((c * tile + s) // LANES, 1), :]
            fq = feat(0, qb[c, :, here])
            sure0 = jnp.concatenate(diag[:2], 0) + brow * mid.astype(F32)
            gate[c, n] = fq[:block] * own_head[pl.ds(0, block)]
            rest[c, n] = fq[:block] * sure0
            fresh = early(tables[c, n], mid, jnp.concatenate([mid[half:], near[:half]], 0), emask.at[2:4], quad)
            sure1 = jnp.concatenate(diag[2:], 0) + brow * near.astype(F32)
            out[block:, at] = (fq[block:] * (sure1 + fresh * own_head[pl.ds(block, block)])).astype(BF16)
            mids[c, :, here] = mid[:half]

    def arrive(c):
        @pl.when(has_left)
        def _():
            product_copy(c).wait_recv()

    @pl.loop(0, tiles - last)
    def _(c):
        arrive(c)
        for s in range(0, tile, LANES):
            out[:block, part(c, s)] = join(
                c, s // LANES, slice(s, s + LANES), halo, mids, tables, gate, rest, emask.at[0:2], quad)

    @pl.loop(tiles - last, tiles)
    def _(c):
        arrive(c)

    @pl.when(has_right)
    def _():
        seg_copy().wait_send()
        edge_copy().wait_send()
        remote(pt, halo, send_sem.at[0], recv_sem.at[0]).wait_send()


def finish(last, members, done, halo, mids, tables, gate, rest, emask, out, fresh, sem):
    rows, width = done.shape
    tiles, block, tile = halo.shape
    half = mids.shape[1]
    quad = quads(half, members)
    ready = width - last * tile
    copies = [
        pltpu.make_async_copy(done.at[at], out.at[at], sem.at[i])
        for i, at in enumerate((
            (pl.ds(0, block), pl.ds(0, ready)),
            (pl.ds(block, half), slice(None)),
            (pl.ds(block + half, half), slice(None))))]
    for copy in copies:
        copy.start()
    for i in range(last):
        c = tiles - last + i
        for s in range(0, tile, LANES):
            here = slice(s, s + LANES)
            fresh[i, :, here] = join(c, s // LANES, here, halo, mids, tables, gate, rest, emask.at[0:2], quad)
        copy = pltpu.make_async_copy(
            fresh.at[i], out.at[pl.ds(0, block), pl.ds(ready + i * tile, tile)], sem.at[3 + i])
        copy.start()
        copies.append(copy)
    for copy in copies:
        copy.wait()


def per_device(queries, keys, values, segments, short_filters, mr_filter, mr_bias):
    rows, width = queries.shape
    block, groups = mr_filter.shape
    half = block // 2
    members = width // groups
    tile = min(TILE, width)
    tiles = width // tile
    parts = tile // LANES
    dma = pltpu.SemaphoreType.DMA
    chunked = lambda r: pltpu.VMEM((tiles, r, tile), BF16)
    last = min(LAST, tiles)
    vmem = pl.BlockSpec(memory_space=pltpu.VMEM)
    held = pl.pallas_call(
        functools.partial(kernel, "tok", members, tiles, last),
        in_specs=[pl.BlockSpec(memory_space=pltpu.HBM)] * 7,
        out_specs=[vmem] * 7,
        out_shape=[
            pltpu.VMEM((rows, width), BF16),
            chunked(block),
            chunked(half),
            pltpu.VMEM((tiles, parts, 4 * half, 2 * block), BF16),
            pltpu.VMEM((tiles, parts, block, LANES), F32),
            pltpu.VMEM((tiles, parts, block, LANES), F32),
            pltpu.VMEM((4, 2, block, LANES), BF16),
        ],
        scratch_shapes=[
            pltpu.VMEM((rows // block, block), jnp.int32),
            pltpu.VMEM(short_filters.shape, BF16),
            pltpu.VMEM(mr_filter.shape, BF16),
            pltpu.VMEM((width // LANES, LANES), BF16),
            chunked(rows),
            pltpu.VMEM((2, tiles, rows, tile), BF16),
            chunked(block),
            pltpu.VMEM((3, 8, width), BF16),
            pltpu.VMEM((3, 2, width), BF16),
            pltpu.VMEM((3, 2, width), BF16),
            pltpu.VMEM((rows // block, block), jnp.int32),
            pltpu.VMEM((groups, block), F32),
            pltpu.VMEM((groups, block), F32),
            pltpu.VMEM((width // LANES, LANES), F32),
            pltpu.VMEM((block + rows, LANES), F32),
            pltpu.VMEM((rows, LANES), F32),
            pltpu.VMEM((rows, LANES), F32),
            pltpu.VMEM((rows, LANES), F32),
            pltpu.VMEM((4, half, LANES), BF16),
            pltpu.VMEM((3, parts, rows + 8, LANES), F32),
            dma((4,)), dma((1,)), dma((tiles,)), dma((tiles,)), dma((tiles,)),
            dma((1,)), dma((tiles,)), dma((2,)), dma((2,)),
        ],
        compiler_params=pltpu.CompilerParams(
            collective_id=0, has_side_effects=True, vmem_limit_bytes=24 * 2**20
        ),
    )(*(pltpu.with_memory_space_constraint(x, pltpu.HBM) for x in (
        queries, keys, values, segments.reshape(rows // block, block), short_filters,
        mr_filter, mr_bias.reshape(width // LANES, LANES))))
    return pl.pallas_call(
        functools.partial(finish, last, members),
        in_specs=[vmem] * 7,
        out_specs=pl.BlockSpec(memory_space=pltpu.HBM),
        out_shape=pltpu.HBM((rows, width), BF16),
        scratch_shapes=[pltpu.VMEM((last, block, tile), BF16), dma((3 + last,))],
        compiler_params=pltpu.CompilerParams(vmem_limit_bytes=8 * 2**20),
    )(*(pltpu.with_memory_space_constraint(x, pltpu.VMEM) for x in held))


def solution(mesh):
    placed = (
        P(("seq", "tok"), None),
        P(("seq", "tok"), None),
        P(("seq", "tok"), None),
        P(("seq", "tok")),
        P(),
        P(),
        P(),
    )
    return jax.shard_map(
        per_device, mesh=mesh, in_specs=placed, out_specs=P(("seq", "tok"), None), check_vma=False
    )
```

```python
import functools

import jax
import jax.numpy as jnp
import numpy as np
from jax import lax
from jax.experimental import pallas as pl
from jax.experimental.pallas import tpu as pltpu
from jax.sharding import PartitionSpec as P

LANES = 128
TILE = 512
LAST = 3
DETOURS = 3
HANDOVER = 5
F32, BF16 = jnp.float32, jnp.bfloat16


def column(row, block):
    return jnp.transpose(jnp.broadcast_to(row, (block, block)))


def quads(half, members):
    return lax.broadcasted_iota(jnp.int32, (half, LANES), 1) // (2 * members)


def early(table, low, high, masks, quad):
    half = quad.shape[0]
    right_side = jnp.concatenate([
        jnp.concatenate([x * masks[j, i] for j, x in enumerate((low, high))], 1)
        for i in range(2)], 0)
    every = jnp.dot(table, right_side, preferred_element_type=F32)
    picked = []
    for j in range(2):
        side = every[:, j * LANES:(j + 1) * LANES]
        parts = [side[h * half:(h + 1) * half] for h in range(4)]
        picked.append(jnp.where(quad == 0, parts[0], jnp.where(
            quad == 1, parts[1], jnp.where(quad == 2, parts[2], parts[3]))))
    return jnp.concatenate(picked, 0)


def join(c, n, here, halo, mids, tables, gate, rest, masks, quad):
    half = quad.shape[0]
    far = halo[c, :, here]
    fresh = early(tables[c, n], far, jnp.concatenate([far[half:], mids[c, :, here]], 0), masks, quad)
    return (gate[c, n] * fresh + rest[c, n]).astype(BF16)


def kernel(axis, members, tiles, last, detours, q, k, v, seg_hbm, taps_hbm, filters_hbm, bias_hbm,
           out, halo, mids, tables, gate, rest, emask,
           seg, taps, filters, bias, qb, kv, pt, raw, edge_send, edge, seg_prev,
           hrev, comb, biasf, segc, one, two, own_head, dmask, wide,
           small_sem, raw_sem, tail_sem, head_sem, q_sem,
           send_sem, recv_sem, small_send, small_recv, passing=None, pass_send=None, pass_recv=None, ready=None):
    rows, width = q.shape
    block = filters.shape[0]
    half = block // 2
    tile = width // tiles
    per = LANES // members
    keep = block - 16
    me = lax.axis_index(axis)
    size = lax.axis_size(axis)
    has_left, has_right = me > 0, me < size - 1
    left, right = jnp.maximum(me - 1, 0), jnp.minimum(me + 1, size - 1)
    turns = (me % 4 == 3) & (me // 4 < detours)
    layer = jnp.minimum(me // 4, max(detours - 1, 0))
    odd_one = tiles - 2
    aside, along = pl.ds(0, tile // 2), pl.ds(tile // 2, tile // 2)
    barrier = pltpu.get_barrier_semaphore()

    def greet(device):
        pl.semaphore_signal(barrier, inc=1, device_id={axis: device}, device_id_type=pl.DeviceIdType.MESH)

    @pl.when(has_left)
    def _():
        greet(left)

    if detours:
        lands = (me % 4 == 0) & (me > 0) & (me // 4 <= detours)

        @pl.when(me == 0)
        def _():
            for z in range(detours):
                greet(4 * z + 3)
                greet(4 * z + 4)

    def cols(c):
        return pl.ds(pl.multiple_of(c * tile, tile), tile)

    def raw_copy(i):
        return pltpu.make_async_copy((q, k, v)[i].at[pl.ds(rows - 8, 8)], raw.at[i], raw_sem.at[0])

    def tail_copy(i, c):
        at = pl.ds(keep, rows - keep)
        return pltpu.make_async_copy((k, v)[i].at[at, cols(c)], kv.at[i, c, at], tail_sem.at[c])

    def head_copy(i, c):
        at = pl.ds(0, keep)
        return pltpu.make_async_copy((k, v)[i].at[at, cols(c)], kv.at[i, c, at], head_sem.at[c])

    def whole(ref, sem):
        return pltpu.make_async_copy(ref, ref, sem)

    def q_copy(c):
        return pltpu.make_async_copy(q.at[:, cols(c)], qb.at[c], q_sem.at[c])

    def remote(src, dst, s, r, device=right):
        return pltpu.make_async_remote_copy(
            src_ref=src, dst_ref=dst, send_sem=s, recv_sem=r,
            device_id={axis: device}, device_id_type=pl.DeviceIdType.MESH)

    def along_copy():
        return remote(pt.at[odd_one, :, along], halo.at[odd_one, :, along], send_sem.at[0], recv_sem.at[odd_one])

    def aside_copy(z):
        return remote(pt.at[odd_one, :, aside], passing.at[z], send_sem.at[0], pass_recv.at[z], 0)

    def onward_copy(z):
        return remote(passing.at[z], halo.at[odd_one, :, aside], pass_send.at[z], recv_sem.at[odd_one], 4 * z + 4)

    def order(i):
        if not detours:
            return i
        return jnp.where(turns, jnp.where(i == 0, odd_one, jnp.where(i <= odd_one, i - 1, i)), i)

    def product_copy(c):
        return remote(pt.at[c], halo.at[c], send_sem.at[0], recv_sem.at[c])

    def edge_copy():
        return remote(edge_send, edge, small_send.at[0], small_recv.at[0])

    def seg_copy():
        return remote(seg, seg_prev, small_send.at[1], small_recv.at[1])

    small = [
        pltpu.make_async_copy(src, dst, small_sem.at[i])
        for i, (src, dst) in enumerate(
            ((seg_hbm, seg), (taps_hbm, taps), (filters_hbm, filters), (bias_hbm, bias)))
    ]
    small[0].start()
    for i in range(3):
        raw_copy(i).start()
    small[1].start()

    @pl.loop(0, tiles)
    def _(i):
        c = order(i)
        tail_copy(0, c).start()
        tail_copy(1, c).start()

    small[2].start()
    small[3].start()

    @pl.loop(0, tiles)
    def _(c):
        head_copy(0, c).start()
        head_copy(1, c).start()
        q_copy(c).start()

    tap = lax.broadcasted_iota(jnp.int32, (half, LANES), 0)
    lane = lax.broadcasted_iota(jnp.int32, (half, LANES), 1)
    strip = lax.broadcasted_iota(jnp.int32, (16, LANES), 1) // members
    pick2 = [(strip % 2 == i).astype(BF16) for i in range(2)]
    pick4 = [(strip % 4 == i).astype(BF16) for i in range(4)]

    def short_masks(at, count):
        here = segc[pl.ds(at + block, count)]
        one[pl.ds(at, count)] = jnp.where(here == segc[pl.ds(at + block - 1, count)], 1.0, 0.0)
        two[pl.ds(at, count)] = jnp.where(here == segc[pl.ds(at + block - 2, count)], 1.0, 0.0)

    def feature(buf, x, lead, taps_rows, at, count):
        buf[pl.ds(lead, x.shape[0])] = x
        first = lead + x.shape[0] - count
        x0 = x[x.shape[0] - count:]
        x1, x2 = buf[pl.ds(first - 1, count)], buf[pl.ds(first - 2, count)]
        return (taps_rows[0:1] * x0 + (taps_rows[1:2] * x1) * one[pl.ds(at, count)]
                + (taps_rows[2:3] * x2) * two[pl.ds(at, count)])

    small[0].wait()
    for b in range(2):
        segc[pl.ds((b + 1) * block, block)] = column(seg[b:b + 1].astype(F32), block)
    short_masks(block, block)
    whole(raw, raw_sem.at[0]).wait()
    for i in range(3):
        edge_send[i] = raw[i].astype(F32)[6:8].astype(BF16)

    def part(c, s):
        return pl.ds(pl.multiple_of(c * tile + s, LANES), LANES)

    def taps_of(i, at):
        return taps[i, :, at].astype(F32)

    small[1].wait()

    @pl.loop(0, tiles)
    def _(step):
        c = order(step)
        whole(kv.at[:, c, pl.ds(keep, rows - keep)], tail_sem.at[c]).wait()
        for s in range(0, tile, LANES):
            at, here = part(c, s), slice(s, s + LANES)
            feats = []
            for i in (1, 2):
                x = kv[i - 1, c, keep:, here].astype(F32)
                feats.append(feature(wide.at[i, s // LANES], x, 8, taps_of(i, at), block, block))
            pt[c, :, here] = (feats[0] * feats[1]).astype(BF16)

        @pl.when(has_right & (step == 0))
        def _():
            if detours:
                pl.semaphore_wait(barrier, jnp.where(turns | lands, 2, 1))

                @pl.when(lands)
                def _():
                    pl.semaphore_signal(
                        ready, inc=1, device_id={axis: 0}, device_id_type=pl.DeviceIdType.MESH)

            else:
                pl.semaphore_wait(barrier, 1)
            seg_copy().start()
            edge_copy().start()

        if detours:
            split = turns & (step == 0)

            @pl.when(split)
            def _():
                aside_copy(layer).start()
                along_copy().start()

            straight = has_right & jnp.logical_not(split)
        else:
            straight = has_right

        @pl.when(straight)
        def _():
            product_copy(c).start()

    small[2].wait()
    small[3].wait()
    wide_tap = lax.broadcasted_iota(jnp.int32, (block, block), 0)
    wide_lane = lax.broadcasted_iota(jnp.int32, (block, block), 1)
    turn = (wide_tap == lax.rem(block - wide_lane, block)).astype(BF16)
    turned = lax.dot_general(
        filters[...], turn, (((0,), (0,)), ((), ())), preferred_element_type=F32)
    hrev[...] = turned
    groups = turned.shape[0]
    glane = lax.broadcasted_iota(jnp.int32, turned.shape, 1)
    comb[...] = jnp.where((glane >= 1) & (glane <= half),
                          pltpu.roll(pltpu.roll(turned, half, 1), groups - 1, 0), turned)
    biasf[...] = bias[...].astype(F32)

    for b in range(4):
        own = segc[pl.ds(block + b * half, half)]
        start = own[0:1]
        own_head[pl.ds(b * half, half)] = jnp.where(own == start, 1.0, 0.0)
        row = seg[b // 2:b // 2 + 1].astype(F32)
        twin = pltpu.roll(jnp.broadcast_to(row, (8, block)), half, 1)[0:1]
        low = lane[0:1] < half
        row = jnp.where(low, row, twin) if b % 2 == 0 else jnp.where(low, twin, row)
        inner = jnp.where(lane < half, lane, lane - half)
        dmask[b] = jnp.where((own == row) & (inner <= tap), 1.0, 0.0).astype(BF16)

    def early_masks(b):
        start = segc[pl.ds(block + b * half, 8)][0:1]
        same = jnp.where(segc[pl.ds(b * half, block)] == start, 1.0, 0.0).astype(BF16)
        for i in range(2):
            emask[b, i] = same * jnp.concatenate([pick2[i]] * (block // 16), 0)

    early_masks(2)
    early_masks(3)
    later = (lane > tap).astype(BF16)

    @pl.when(has_left)
    def _():
        seg_copy().wait_recv()
        edge_copy().wait_recv()

    @pl.when(jnp.logical_not(has_left))
    def _():
        seg_prev[...] = jnp.zeros_like(seg_prev)
        edge[...] = jnp.zeros_like(edge)

        @pl.loop(0, tiles)
        def _(c):
            halo[c] = jnp.zeros_like(halo[c])

    segc[pl.ds(0, block)] = column(seg_prev[1:2].astype(F32), block)
    short_masks(0, block)
    early_masks(0)
    early_masks(1)

    quad = quads(half, members)

    @pl.loop(0, tiles)
    def _(c):
        if detours:
            @pl.when((me == 0) & (c == HANDOVER * tiles // 8))
            def _():
                pl.semaphore_wait(ready, detours)
                for z in reversed(range(detours)):
                    aside_copy(z).wait_recv()
                    onward_copy(z).start()

        whole(kv.at[:, c, pl.ds(0, keep)], head_sem.at[c]).wait()
        q_copy(c).wait()
        for s in range(0, tile, LANES):
            at, here, n = part(c, s), slice(s, s + LANES), s // LANES

            def feat(i, x):
                wide[i, n, pl.ds(6, 2)] = edge[i, :, at].astype(F32)
                return feature(wide.at[i, n], x.astype(F32), 8, taps_of(i, at), 0, x.shape[0])

            mid = (feat(1, kv[0, c, :block, here]) * feat(2, kv[1, c, :block, here])).astype(BF16)
            near = pt[c, :, here]
            first = (c * tile + s) // members

            def ring(source, g):
                base = jnp.broadcast_to(source[pl.ds(first + g, 1), :], (half, block))
                return pltpu.roll(base, 0, 1, stride=1, stride_axis=0).astype(BF16)

            for h in range(4):
                for i in range(2):
                    tables[c, n, h * half:(h + 1) * half, i * block:(i + 1) * block] = ring(hrev, 2 * h + i) * later
            own = [[ring(comb, 4 * h + 2 * i) for i in range(2)] for h in range(2)]
            blocks = (mid[:half], mid[half:], near[:half], near[half:])
            diag = []
            for b in range(4):
                left_side = jnp.concatenate([
                    jnp.concatenate([own[h][i] * dmask[b] for i in range(2)], 1) for h in range(2)], 0)
                right_side = jnp.concatenate([
                    blocks[b] * jnp.concatenate([pick4[i]] * (half // 16), 0) for i in range(4)], 0)
                every = jnp.dot(left_side, right_side, preferred_element_type=F32)
                diag.append(jnp.where(quad < 2, every[:half], every[half:]))
            brow = biasf[pl.ds((c * tile + s) // LANES, 1), :]
            fq = feat(0, qb[c, :, here])
            sure0 = jnp.concatenate(diag[:2], 0) + brow * mid.astype(F32)
            gate[c, n] = fq[:block] * own_head[pl.ds(0, block)]
            rest[c, n] = fq[:block] * sure0
            fresh = early(tables[c, n], mid, jnp.concatenate([mid[half:], near[:half]], 0), emask.at[2:4], quad)
            sure1 = jnp.concatenate(diag[2:], 0) + brow * near.astype(F32)
            out[block:, at] = (fq[block:] * (sure1 + fresh * own_head[pl.ds(block, block)])).astype(BF16)
            mids[c, :, here] = mid[:half]

    def arrive(c):
        @pl.when(has_left)
        def _():
            product_copy(c).wait_recv()

    @pl.loop(0, tiles - last)
    def _(c):
        arrive(c)
        for s in range(0, tile, LANES):
            out[:block, part(c, s)] = join(
                c, s // LANES, slice(s, s + LANES), halo, mids, tables, gate, rest, emask.at[0:2], quad)

    @pl.loop(tiles - last, tiles)
    def _(c):
        arrive(c)

    @pl.when(has_right)
    def _():
        seg_copy().wait_send()
        edge_copy().wait_send()
        remote(pt, halo, send_sem.at[0], recv_sem.at[0]).wait_send()

    if detours:
        @pl.when(me == 0)
        def _():
            for z in range(detours):
                onward_copy(z).wait_send()


def finish(last, members, done, halo, mids, tables, gate, rest, emask, out, fresh, sem):
    rows, width = done.shape
    tiles, block, tile = halo.shape
    half = mids.shape[1]
    quad = quads(half, members)
    ready = width - last * tile
    copies = [
        pltpu.make_async_copy(done.at[at], out.at[at], sem.at[i])
        for i, at in enumerate((
            (pl.ds(0, block), pl.ds(0, ready)),
            (pl.ds(block, half), slice(None)),
            (pl.ds(block + half, half), slice(None))))]
    for copy in copies:
        copy.start()
    for i in range(last):
        c = tiles - last + i
        for s in range(0, tile, LANES):
            here = slice(s, s + LANES)
            fresh[i, :, here] = join(c, s // LANES, here, halo, mids, tables, gate, rest, emask.at[0:2], quad)
        copy = pltpu.make_async_copy(
            fresh.at[i], out.at[pl.ds(0, block), pl.ds(ready + i * tile, tile)], sem.at[3 + i])
        copy.start()
        copies.append(copy)
    for copy in copies:
        copy.wait()


def layers_of(mesh, axis):
    at = mesh.axis_names.index(axis)
    lines = np.moveaxis(mesh.devices, at, -1).reshape(-1, mesh.shape[axis])
    if lines.shape[1] % 4:
        return 1
    for line in lines:
        spots = [getattr(d, "coords", None) for d in line]
        if None in spots:
            return 1
        spots = np.array([tuple(spot) for spot in spots])
        spots = spots - spots[0]
        chip = np.arange(len(line)) // 2
        want = np.stack([np.zeros_like(chip), chip % 2, chip // 2], 1)
        if not np.array_equal(spots, want):
            return 1
    return lines.shape[1] // 4


def per_device(layers, queries, keys, values, segments, short_filters, mr_filter, mr_bias):
    rows, width = queries.shape
    block, groups = mr_filter.shape
    half = block // 2
    members = width // groups
    tile = min(TILE, width)
    tiles = width // tile
    parts = tile // LANES
    dma = pltpu.SemaphoreType.DMA
    chunked = lambda r: pltpu.VMEM((tiles, r, tile), BF16)
    last = min(LAST, tiles)
    detours = min(DETOURS, layers - 1) if tiles > 1 else 0
    vmem = pl.BlockSpec(memory_space=pltpu.VMEM)
    held = pl.pallas_call(
        functools.partial(kernel, "tok", members, tiles, last, detours),
        in_specs=[pl.BlockSpec(memory_space=pltpu.HBM)] * 7,
        out_specs=[vmem] * 7,
        out_shape=[
            pltpu.VMEM((rows, width), BF16),
            chunked(block),
            chunked(half),
            pltpu.VMEM((tiles, parts, 4 * half, 2 * block), BF16),
            pltpu.VMEM((tiles, parts, block, LANES), F32),
            pltpu.VMEM((tiles, parts, block, LANES), F32),
            pltpu.VMEM((4, 2, block, LANES), BF16),
        ],
        scratch_shapes=[
            pltpu.VMEM((rows // block, block), jnp.int32),
            pltpu.VMEM(short_filters.shape, BF16),
            pltpu.VMEM(mr_filter.shape, BF16),
            pltpu.VMEM((width // LANES, LANES), BF16),
            chunked(rows),
            pltpu.VMEM((2, tiles, rows, tile), BF16),
            chunked(block),
            pltpu.VMEM((3, 8, width), BF16),
            pltpu.VMEM((3, 2, width), BF16),
            pltpu.VMEM((3, 2, width), BF16),
            pltpu.VMEM((rows // block, block), jnp.int32),
            pltpu.VMEM((groups, block), F32),
            pltpu.VMEM((groups, block), F32),
            pltpu.VMEM((width // LANES, LANES), F32),
            pltpu.VMEM((block + rows, LANES), F32),
            pltpu.VMEM((rows, LANES), F32),
            pltpu.VMEM((rows, LANES), F32),
            pltpu.VMEM((rows, LANES), F32),
            pltpu.VMEM((4, half, LANES), BF16),
            pltpu.VMEM((3, parts, rows + 8, LANES), F32),
            dma((4,)), dma((1,)), dma((tiles,)), dma((tiles,)), dma((tiles,)),
            dma((1,)), dma((tiles,)), dma((2,)), dma((2,)),
        ] + ([
            pltpu.VMEM((detours, block, tile // 2), BF16), dma((detours,)), dma((detours,)),
            pltpu.SemaphoreType.REGULAR,
        ] if detours else []),
        compiler_params=pltpu.CompilerParams(
            collective_id=0, has_side_effects=True, vmem_limit_bytes=24 * 2**20
        ),
    )(*(pltpu.with_memory_space_constraint(x, pltpu.HBM) for x in (
        queries, keys, values, segments.reshape(rows // block, block), short_filters,
        mr_filter, mr_bias.reshape(width // LANES, LANES))))
    return pl.pallas_call(
        functools.partial(finish, last, members),
        in_specs=[vmem] * 7,
        out_specs=pl.BlockSpec(memory_space=pltpu.HBM),
        out_shape=pltpu.HBM((rows, width), BF16),
        scratch_shapes=[pltpu.VMEM((last, block, tile), BF16), dma((3 + last,))],
        compiler_params=pltpu.CompilerParams(vmem_limit_bytes=8 * 2**20),
    )(*(pltpu.with_memory_space_constraint(x, pltpu.VMEM) for x in held))


def solution(mesh):
    placed = (
        P(("seq", "tok"), None),
        P(("seq", "tok"), None),
        P(("seq", "tok"), None),
        P(("seq", "tok")),
        P(),
        P(),
        P(),
    )
    return jax.shard_map(
        functools.partial(per_device, layers_of(mesh, "tok")), mesh=mesh, in_specs=placed, out_specs=P(("seq", "tok"), None), check_vma=False
    )
```

```python
import functools

import jax
import jax.numpy as jnp
import numpy as np
from jax import lax
from jax.experimental import pallas as pl
from jax.experimental.pallas import tpu as pltpu
from jax.sharding import PartitionSpec as P

LANES = 128
TILE = 512
LAST = 3
DETOURS = 3
HANDOVER = 5
F32, BF16 = jnp.float32, jnp.bfloat16


def column(row, block):
    return jnp.transpose(jnp.broadcast_to(row, (block, block)))


def cuts_of(tiles, last):
    inner = tiles - last
    return [0] + [n for n in (1, 3) if n < inner] + ([inner] if inner else []) + [tiles]


def quads(half, members):
    return lax.broadcasted_iota(jnp.int32, (half, LANES), 1) // (2 * members)


def early(table, low, high, masks, quad):
    half = quad.shape[0]
    right_side = jnp.concatenate([
        jnp.concatenate([x * masks[j, i] for j, x in enumerate((low, high))], 1)
        for i in range(2)], 0)
    every = jnp.dot(table, right_side, preferred_element_type=F32)
    picked = []
    for j in range(2):
        side = every[:, j * LANES:(j + 1) * LANES]
        parts = [side[h * half:(h + 1) * half] for h in range(4)]
        picked.append(jnp.where(quad == 0, parts[0], jnp.where(
            quad == 1, parts[1], jnp.where(quad == 2, parts[2], parts[3]))))
    return jnp.concatenate(picked, 0)


def join(c, n, here, halo, mids, tables, gate, rest, masks, quad):
    half = quad.shape[0]
    far = halo[c, :, here]
    fresh = early(tables[c, n], far, jnp.concatenate([far[half:], mids[c, :, here]], 0), masks, quad)
    return (gate[c, n] * fresh + rest[c, n]).astype(BF16)


def kernel(axis, members, tiles, last, detours, q, k, v, seg_hbm, taps_hbm, filters_hbm, bias_hbm,
           out, halo, mids, tables, gate, rest, emask,
           seg, taps, filters, bias, qb, kv, pt, raw, edge_send, edge,
           hrev, comb, biasf, segc, one, two, own_head, dmask, wide,
           small_sem, raw_sem, tail_sem, head_sem, q_sem,
           send_sem, recv_sem, small_send, small_recv, passing=None, pass_send=None, pass_recv=None, ready=None):
    rows, width = q.shape
    block = filters.shape[0]
    half = block // 2
    tile = width // tiles
    per = LANES // members
    keep = block - 16
    me = lax.axis_index(axis)
    size = lax.axis_size(axis)
    has_left, has_right = me > 0, me < size - 1
    left, right = jnp.maximum(me - 1, 0), jnp.minimum(me + 1, size - 1)
    turns = (me % 4 == 3) & (me // 4 < detours)
    layer = jnp.minimum(me // 4, max(detours - 1, 0))
    cuts = cuts_of(tiles, last)
    odd_one = cuts[-2]
    wide_part = tile // 4 * 3
    aside, along = pl.ds(0, wide_part), pl.ds(wide_part, tile - wide_part)
    barrier = pltpu.get_barrier_semaphore()

    def greet(device):
        pl.semaphore_signal(barrier, inc=1, device_id={axis: device}, device_id_type=pl.DeviceIdType.MESH)

    @pl.when(has_left)
    def _():
        greet(left)

    if detours:
        lands = (me % 4 == 0) & (me > 0) & (me // 4 <= detours)

        @pl.when(me == 0)
        def _():
            for z in range(detours):
                greet(4 * z + 3)
                greet(4 * z + 4)

    def cols(c):
        return pl.ds(pl.multiple_of(c * tile, tile), tile)

    def raw_copy(i):
        return pltpu.make_async_copy((q, k, v)[i].at[pl.ds(rows - 8, 8)], raw.at[i], raw_sem.at[0])

    def tail_copy(i, c):
        at = pl.ds(keep, rows - keep)
        return pltpu.make_async_copy((k, v)[i].at[at, cols(c)], kv.at[i, c, at], tail_sem.at[c])

    def head_copy(i, c):
        at = pl.ds(0, keep)
        return pltpu.make_async_copy((k, v)[i].at[at, cols(c)], kv.at[i, c, at], head_sem.at[c])

    def whole(ref, sem):
        return pltpu.make_async_copy(ref, ref, sem)

    def q_copy(c):
        return pltpu.make_async_copy(q.at[:, cols(c)], qb.at[c], q_sem.at[c])

    def remote(src, dst, s, r, device=right):
        return pltpu.make_async_remote_copy(
            src_ref=src, dst_ref=dst, send_sem=s, recv_sem=r,
            device_id={axis: device}, device_id_type=pl.DeviceIdType.MESH)

    def along_copy():
        return remote(pt.at[odd_one, :, along], halo.at[odd_one, :, along], send_sem.at[0], recv_sem.at[len(cuts) - 2])

    def aside_copy(z):
        return remote(pt.at[odd_one, :, aside], passing.at[z], send_sem.at[0], pass_recv.at[z], 0)

    def onward_copy(z):
        return remote(passing.at[z], halo.at[odd_one, :, aside], pass_send.at[z], recv_sem.at[len(cuts) - 2], 4 * z + 4)

    def order(i):
        return jnp.where(i == 0, odd_one, jnp.where(i <= odd_one, i - 1, i))

    def part_copy(g, skip=0):
        at = pl.ds(cuts[g] + skip, cuts[g + 1] - cuts[g] - skip)
        return remote(pt.at[at], halo.at[at], send_sem.at[0], recv_sem.at[g])

    def edge_copy():
        return remote(edge_send, edge, small_send.at[0], small_recv.at[0])

    small = [
        pltpu.make_async_copy(src, dst, small_sem.at[i])
        for i, (src, dst) in enumerate(
            ((seg_hbm, seg), (taps_hbm, taps), (filters_hbm, filters), (bias_hbm, bias)))
    ]
    small[0].start()
    for i in range(3):
        raw_copy(i).start()
    small[1].start()

    @pl.loop(0, tiles)
    def _(i):
        c = order(i)
        tail_copy(0, c).start()
        tail_copy(1, c).start()

    small[2].start()
    small[3].start()

    @pl.loop(0, tiles)
    def _(c):
        head_copy(0, c).start()
        head_copy(1, c).start()
        q_copy(c).start()

    tap = lax.broadcasted_iota(jnp.int32, (half, LANES), 0)
    lane = lax.broadcasted_iota(jnp.int32, (half, LANES), 1)
    strip = lax.broadcasted_iota(jnp.int32, (16, LANES), 1) // members
    pick2 = [(strip % 2 == i).astype(BF16) for i in range(2)]
    pick4 = [(strip % 4 == i).astype(BF16) for i in range(4)]

    def short_masks(at, count):
        here = segc[pl.ds(at + block, count)]
        one[pl.ds(at, count)] = jnp.where(here == segc[pl.ds(at + block - 1, count)], 1.0, 0.0)
        two[pl.ds(at, count)] = jnp.where(here == segc[pl.ds(at + block - 2, count)], 1.0, 0.0)

    def feature(buf, x, lead, taps_rows, at, count):
        buf[pl.ds(lead, x.shape[0])] = x
        first = lead + x.shape[0] - count
        x0 = x[x.shape[0] - count:]
        x1, x2 = buf[pl.ds(first - 1, count)], buf[pl.ds(first - 2, count)]
        return (taps_rows[0:1] * x0 + (taps_rows[1:2] * x1) * one[pl.ds(at, count)]
                + (taps_rows[2:3] * x2) * two[pl.ds(at, count)])

    small[0].wait()
    for b in range(2):
        segc[pl.ds((b + 1) * block, block)] = column(seg[b:b + 1].astype(F32), block)
    short_masks(block, block)
    whole(raw, raw_sem.at[0]).wait()
    for i in range(3):
        edge_send[i, :, :width] = raw[i].astype(F32)[6:8].astype(BF16)
    edge_send[0, :, width:] = jnp.broadcast_to(seg[1:2].astype(F32), (2, block)).astype(BF16)
    for i in (1, 2):
        edge_send[i, :, width:] = jnp.zeros((2, block), BF16)

    def part(c, s):
        return pl.ds(pl.multiple_of(c * tile + s, LANES), LANES)

    def taps_of(i, at):
        return taps[i, :, at].astype(F32)

    small[1].wait()

    def produce(step):
        c = order(step)
        whole(kv.at[:, c, pl.ds(keep, rows - keep)], tail_sem.at[c]).wait()
        for s in range(0, tile, LANES):
            at, here = part(c, s), slice(s, s + LANES)
            feats = []
            for i in (1, 2):
                x = kv[i - 1, c, keep:, here].astype(F32)
                feats.append(feature(wide.at[i, s // LANES], x, 8, taps_of(i, at), block, block))
            pt[c, :, here] = (feats[0] * feats[1]).astype(BF16)

    def open_link():
        if not detours:
            pl.semaphore_wait(barrier, 1)
            edge_copy().start()
            return
        pl.semaphore_wait(barrier, jnp.where(turns | lands, 2, 1))
        edge_copy().start()

        @pl.when(lands)
        def _():
            pl.semaphore_signal(ready, inc=1, device_id={axis: 0}, device_id_type=pl.DeviceIdType.MESH)

        @pl.when(turns)
        def _():
            aside_copy(layer).start()
            along_copy().start()

    begin = 0
    for g in range(len(cuts) - 1):
        final = g == len(cuts) - 2
        end = tiles if final else cuts[g + 1] + 1
        pl.loop(begin, end)(produce)
        begin = end

        @pl.when(has_right)
        def _():
            if g == 0:
                open_link()
            if not (final and detours):
                part_copy(g).start()
                return

            @pl.when(turns)
            def _():
                part_copy(g, 1).start()

            @pl.when(jnp.logical_not(turns))
            def _():
                part_copy(g).start()

    small[2].wait()
    small[3].wait()
    wide_tap = lax.broadcasted_iota(jnp.int32, (block, block), 0)
    wide_lane = lax.broadcasted_iota(jnp.int32, (block, block), 1)
    turn = (wide_tap == lax.rem(block - wide_lane, block)).astype(BF16)
    turned = lax.dot_general(
        filters[...], turn, (((0,), (0,)), ((), ())), preferred_element_type=F32)
    hrev[...] = turned
    groups = turned.shape[0]
    glane = lax.broadcasted_iota(jnp.int32, turned.shape, 1)
    comb[...] = jnp.where((glane >= 1) & (glane <= half),
                          pltpu.roll(pltpu.roll(turned, half, 1), groups - 1, 0), turned)
    biasf[...] = bias[...].astype(F32)

    for b in range(4):
        own = segc[pl.ds(block + b * half, half)]
        start = own[0:1]
        own_head[pl.ds(b * half, half)] = jnp.where(own == start, 1.0, 0.0)
        row = seg[b // 2:b // 2 + 1].astype(F32)
        twin = pltpu.roll(jnp.broadcast_to(row, (8, block)), half, 1)[0:1]
        low = lane[0:1] < half
        row = jnp.where(low, row, twin) if b % 2 == 0 else jnp.where(low, twin, row)
        inner = jnp.where(lane < half, lane, lane - half)
        dmask[b] = jnp.where((own == row) & (inner <= tap), 1.0, 0.0).astype(BF16)

    def early_masks(b):
        start = segc[pl.ds(block + b * half, 8)][0:1]
        same = jnp.where(segc[pl.ds(b * half, block)] == start, 1.0, 0.0).astype(BF16)
        for i in range(2):
            emask[b, i] = same * jnp.concatenate([pick2[i]] * (block // 16), 0)

    early_masks(2)
    early_masks(3)
    later = (lane > tap).astype(BF16)

    @pl.when(has_left)
    def _():
        edge_copy().wait_recv()

    @pl.when(jnp.logical_not(has_left))
    def _():
        edge[...] = jnp.zeros_like(edge)

        @pl.loop(0, tiles)
        def _(c):
            halo[c] = jnp.zeros_like(halo[c])

    segc[pl.ds(0, block)] = column(edge[0, :, width:].astype(F32)[0:1], block)
    short_masks(0, block)
    early_masks(0)
    early_masks(1)

    quad = quads(half, members)

    @pl.loop(0, tiles)
    def _(c):
        if detours:
            @pl.when((me == 0) & (c == HANDOVER * tiles // 8))
            def _():
                pl.semaphore_wait(ready, detours)
                for z in reversed(range(detours)):
                    aside_copy(z).wait_recv()
                    onward_copy(z).start()

        whole(kv.at[:, c, pl.ds(0, keep)], head_sem.at[c]).wait()
        q_copy(c).wait()
        for s in range(0, tile, LANES):
            at, here, n = part(c, s), slice(s, s + LANES), s // LANES

            def feat(i, x):
                wide[i, n, pl.ds(6, 2)] = edge[i, :, at].astype(F32)
                return feature(wide.at[i, n], x.astype(F32), 8, taps_of(i, at), 0, x.shape[0])

            mid = (feat(1, kv[0, c, :block, here]) * feat(2, kv[1, c, :block, here])).astype(BF16)
            near = pt[c, :, here]
            first = (c * tile + s) // members

            def ring(source, g):
                base = jnp.broadcast_to(source[pl.ds(first + g, 1), :], (half, block))
                return pltpu.roll(base, 0, 1, stride=1, stride_axis=0).astype(BF16)

            for h in range(4):
                for i in range(2):
                    tables[c, n, h * half:(h + 1) * half, i * block:(i + 1) * block] = ring(hrev, 2 * h + i) * later
            own = [[ring(comb, 4 * h + 2 * i) for i in range(2)] for h in range(2)]
            blocks = (mid[:half], mid[half:], near[:half], near[half:])
            diag = []
            for b in range(4):
                left_side = jnp.concatenate([
                    jnp.concatenate([own[h][i] * dmask[b] for i in range(2)], 1) for h in range(2)], 0)
                right_side = jnp.concatenate([
                    blocks[b] * jnp.concatenate([pick4[i]] * (half // 16), 0) for i in range(4)], 0)
                every = jnp.dot(left_side, right_side, preferred_element_type=F32)
                diag.append(jnp.where(quad < 2, every[:half], every[half:]))
            brow = biasf[pl.ds((c * tile + s) // LANES, 1), :]
            fq = feat(0, qb[c, :, here])
            sure0 = jnp.concatenate(diag[:2], 0) + brow * mid.astype(F32)
            gate[c, n] = fq[:block] * own_head[pl.ds(0, block)]
            rest[c, n] = fq[:block] * sure0
            fresh = early(tables[c, n], mid, jnp.concatenate([mid[half:], near[:half]], 0), emask.at[2:4], quad)
            sure1 = jnp.concatenate(diag[2:], 0) + brow * near.astype(F32)
            out[block:, at] = (fq[block:] * (sure1 + fresh * own_head[pl.ds(block, block)])).astype(BF16)
            mids[c, :, here] = mid[:half]

    @pl.loop(0, tiles - last)
    def _(c):
        for g in range(len(cuts) - 2):
            @pl.when(has_left & (c == cuts[g]))
            def _():
                part_copy(g).wait_recv()

        for s in range(0, tile, LANES):
            out[:block, part(c, s)] = join(
                c, s // LANES, slice(s, s + LANES), halo, mids, tables, gate, rest, emask.at[0:2], quad)

    @pl.when(has_left)
    def _():
        part_copy(len(cuts) - 2).wait_recv()

    @pl.when(has_right)
    def _():
        edge_copy().wait_send()
        remote(pt, halo, send_sem.at[0], recv_sem.at[0]).wait_send()

    if detours:
        @pl.when(me == 0)
        def _():
            for z in range(detours):
                onward_copy(z).wait_send()


def finish(last, members, done, halo, mids, tables, gate, rest, emask, out, fresh, sem):
    rows, width = done.shape
    tiles, block, tile = halo.shape
    half = mids.shape[1]
    quad = quads(half, members)
    ready = width - last * tile
    copies = [
        pltpu.make_async_copy(done.at[at], out.at[at], sem.at[i])
        for i, at in enumerate((
            (pl.ds(0, block), pl.ds(0, ready)),
            (pl.ds(block, half), slice(None)),
            (pl.ds(block + half, half), slice(None))))]
    for copy in copies:
        copy.start()
    for i in range(last):
        c = tiles - last + i
        for s in range(0, tile, LANES):
            here = slice(s, s + LANES)
            fresh[i, :, here] = join(c, s // LANES, here, halo, mids, tables, gate, rest, emask.at[0:2], quad)
        copy = pltpu.make_async_copy(
            fresh.at[i], out.at[pl.ds(0, block), pl.ds(ready + i * tile, tile)], sem.at[3 + i])
        copy.start()
        copies.append(copy)
    for copy in copies:
        copy.wait()


def layers_of(mesh, axis):
    at = mesh.axis_names.index(axis)
    lines = np.moveaxis(mesh.devices, at, -1).reshape(-1, mesh.shape[axis])
    if lines.shape[1] % 4:
        return 1
    for line in lines:
        spots = [getattr(d, "coords", None) for d in line]
        if None in spots:
            return 1
        spots = np.array([tuple(spot) for spot in spots])
        spots = spots - spots[0]
        chip = np.arange(len(line)) // 2
        want = np.stack([np.zeros_like(chip), chip % 2, chip // 2], 1)
        if not np.array_equal(spots, want):
            return 1
    return lines.shape[1] // 4


def per_device(layers, queries, keys, values, segments, short_filters, mr_filter, mr_bias):
    rows, width = queries.shape
    block, groups = mr_filter.shape
    half = block // 2
    members = width // groups
    tile = min(TILE, width)
    tiles = width // tile
    parts = tile // LANES
    dma = pltpu.SemaphoreType.DMA
    chunked = lambda r: pltpu.VMEM((tiles, r, tile), BF16)
    last = min(LAST, tiles)
    detours = min(DETOURS, layers - 1) if tiles > 1 else 0
    vmem = pl.BlockSpec(memory_space=pltpu.VMEM)
    held = pl.pallas_call(
        functools.partial(kernel, "tok", members, tiles, last, detours),
        in_specs=[pl.BlockSpec(memory_space=pltpu.HBM)] * 7,
        out_specs=[vmem] * 7,
        out_shape=[
            pltpu.VMEM((rows, width), BF16),
            chunked(block),
            chunked(half),
            pltpu.VMEM((tiles, parts, 4 * half, 2 * block), BF16),
            pltpu.VMEM((tiles, parts, block, LANES), F32),
            pltpu.VMEM((tiles, parts, block, LANES), F32),
            pltpu.VMEM((4, 2, block, LANES), BF16),
        ],
        scratch_shapes=[
            pltpu.VMEM((rows // block, block), jnp.int32),
            pltpu.VMEM(short_filters.shape, BF16),
            pltpu.VMEM(mr_filter.shape, BF16),
            pltpu.VMEM((width // LANES, LANES), BF16),
            chunked(rows),
            pltpu.VMEM((2, tiles, rows, tile), BF16),
            chunked(block),
            pltpu.VMEM((3, 8, width), BF16),
            pltpu.VMEM((3, 2, width + block), BF16),
            pltpu.VMEM((3, 2, width + block), BF16),
            pltpu.VMEM((groups, block), F32),
            pltpu.VMEM((groups, block), F32),
            pltpu.VMEM((width // LANES, LANES), F32),
            pltpu.VMEM((block + rows, LANES), F32),
            pltpu.VMEM((rows, LANES), F32),
            pltpu.VMEM((rows, LANES), F32),
            pltpu.VMEM((rows, LANES), F32),
            pltpu.VMEM((4, half, LANES), BF16),
            pltpu.VMEM((3, parts, rows + 8, LANES), F32),
            dma((4,)), dma((1,)), dma((tiles,)), dma((tiles,)), dma((tiles,)),
            dma((1,)), dma((len(cuts_of(tiles, last)) - 1,)), dma((1,)), dma((1,)),
        ] + ([
            pltpu.VMEM((detours, block, tile // 4 * 3), BF16), dma((detours,)), dma((detours,)),
            pltpu.SemaphoreType.REGULAR,
        ] if detours else []),
        compiler_params=pltpu.CompilerParams(
            collective_id=0, has_side_effects=True, vmem_limit_bytes=24 * 2**20
        ),
    )(*(pltpu.with_memory_space_constraint(x, pltpu.HBM) for x in (
        queries, keys, values, segments.reshape(rows // block, block), short_filters,
        mr_filter, mr_bias.reshape(width // LANES, LANES))))
    return pl.pallas_call(
        functools.partial(finish, last, members),
        in_specs=[vmem] * 7,
        out_specs=pl.BlockSpec(memory_space=pltpu.HBM),
        out_shape=pltpu.HBM((rows, width), BF16),
        scratch_shapes=[pltpu.VMEM((last, block, tile), BF16), dma((3 + last,))],
        compiler_params=pltpu.CompilerParams(vmem_limit_bytes=8 * 2**20),
    )(*(pltpu.with_memory_space_constraint(x, pltpu.VMEM) for x in held))


def solution(mesh):
    placed = (
        P(("seq", "tok"), None),
        P(("seq", "tok"), None),
        P(("seq", "tok"), None),
        P(("seq", "tok")),
        P(),
        P(),
        P(),
    )
    return jax.shard_map(
        functools.partial(per_device, layers_of(mesh, "tok")), mesh=mesh, in_specs=placed, out_specs=P(("seq", "tok"), None), check_vma=False
    )
```

```python
import functools

import jax
import jax.numpy as jnp
import numpy as np
from jax import lax
from jax.experimental import pallas as pl
from jax.experimental.pallas import tpu as pltpu
from jax.sharding import PartitionSpec as P

LANES = 128
TILE = 512
LAST = 3
DETOURS = 3
HANDOVER = 5
F32, BF16 = jnp.float32, jnp.bfloat16


def column(row, block):
    return jnp.transpose(jnp.broadcast_to(row, (block, block)))


def cuts_of(tiles, last):
    inner = tiles - last
    return [0] + [n for n in (1,) if n < inner] + ([inner] if inner else []) + [tiles]


def quads(half, members):
    return lax.broadcasted_iota(jnp.int32, (half, LANES), 1) // (2 * members)


def early(table, low, high, masks, quad):
    half = quad.shape[0]
    right_side = jnp.concatenate([
        jnp.concatenate([x * masks[j, i] for j, x in enumerate((low, high))], 1)
        for i in range(2)], 0)
    every = jnp.dot(table, right_side, preferred_element_type=F32)
    picked = []
    for j in range(2):
        side = every[:, j * LANES:(j + 1) * LANES]
        parts = [side[h * half:(h + 1) * half] for h in range(4)]
        picked.append(jnp.where(quad == 0, parts[0], jnp.where(
            quad == 1, parts[1], jnp.where(quad == 2, parts[2], parts[3]))))
    return jnp.concatenate(picked, 0)


def join(c, n, here, halo, mids, tables, gate, rest, masks, quad):
    half = quad.shape[0]
    far = halo[c, :, here]
    fresh = early(tables[c, n], far, jnp.concatenate([far[half:], mids[c, :, here]], 0), masks, quad)
    return (gate[c, n] * fresh + rest[c, n]).astype(BF16)


def kernel(axis, members, tiles, last, detours, q, k, v, seg_hbm, taps_hbm, filters_hbm, bias_hbm,
           out, halo, mids, tables, gate, rest, emask,
           seg, taps, filters, bias, qb, kv, pt, raw, edge_send, edge,
           hrev, comb, biasf, segc, one, two, own_head, dmask, wide,
           small_sem, raw_sem, tail_sem, head_sem, q_sem,
           send_sem, recv_sem, small_send, small_recv, passing=None, pass_send=None, pass_recv=None, ready=None):
    rows, width = q.shape
    block = filters.shape[0]
    half = block // 2
    tile = width // tiles
    per = LANES // members
    keep = block - 16
    me = lax.axis_index(axis)
    size = lax.axis_size(axis)
    has_left, has_right = me > 0, me < size - 1
    left, right = jnp.maximum(me - 1, 0), jnp.minimum(me + 1, size - 1)
    turns = (me % 4 == 3) & (me // 4 < detours)
    layer = jnp.minimum(me // 4, max(detours - 1, 0))
    cuts = cuts_of(tiles, last)
    odd_one = cuts[-2]
    wide_part = tile // 4 * 3
    aside, along = pl.ds(0, wide_part), pl.ds(wide_part, tile - wide_part)
    barrier = pltpu.get_barrier_semaphore()

    def greet(device):
        pl.semaphore_signal(barrier, inc=1, device_id={axis: device}, device_id_type=pl.DeviceIdType.MESH)

    @pl.when(has_left)
    def _():
        greet(left)

    if detours:
        lands = (me % 4 == 0) & (me > 0) & (me // 4 <= detours)

        @pl.when(me == 0)
        def _():
            for z in range(detours):
                greet(4 * z + 3)
                greet(4 * z + 4)

    def cols(c):
        return pl.ds(pl.multiple_of(c * tile, tile), tile)

    def raw_copy(i):
        return pltpu.make_async_copy((q, k, v)[i].at[pl.ds(rows - 8, 8)], raw.at[i], raw_sem.at[0])

    def tail_copy(i, c):
        at = pl.ds(keep, rows - keep)
        return pltpu.make_async_copy((k, v)[i].at[at, cols(c)], kv.at[i, c, at], tail_sem.at[c])

    def head_copy(i, c):
        at = pl.ds(0, keep)
        return pltpu.make_async_copy((k, v)[i].at[at, cols(c)], kv.at[i, c, at], head_sem.at[c])

    def whole(ref, sem):
        return pltpu.make_async_copy(ref, ref, sem)

    def q_copy(c):
        return pltpu.make_async_copy(q.at[:, cols(c)], qb.at[c], q_sem.at[c])

    def remote(src, dst, s, r, device=right):
        return pltpu.make_async_remote_copy(
            src_ref=src, dst_ref=dst, send_sem=s, recv_sem=r,
            device_id={axis: device}, device_id_type=pl.DeviceIdType.MESH)

    def along_copy():
        return remote(pt.at[odd_one, :, along], halo.at[odd_one, :, along], send_sem.at[0], recv_sem.at[len(cuts) - 2])

    def aside_copy(z):
        return remote(pt.at[odd_one, :, aside], passing.at[z], send_sem.at[0], pass_recv.at[z], 0)

    def onward_copy(z):
        return remote(passing.at[z], halo.at[odd_one, :, aside], pass_send.at[z], recv_sem.at[len(cuts) - 2], 4 * z + 4)

    def order(i):
        return jnp.where(i == 0, odd_one, jnp.where(i <= odd_one, i - 1, i))

    def part_copy(g, skip=0):
        at = pl.ds(cuts[g] + skip, cuts[g + 1] - cuts[g] - skip)
        return remote(pt.at[at], halo.at[at], send_sem.at[0], recv_sem.at[g])

    def edge_copy():
        return remote(edge_send, edge, small_send.at[0], small_recv.at[0])

    small = [
        pltpu.make_async_copy(src, dst, small_sem.at[i])
        for i, (src, dst) in enumerate(
            ((seg_hbm, seg), (taps_hbm, taps), (filters_hbm, filters), (bias_hbm, bias)))
    ]
    small[0].start()
    for i in range(3):
        raw_copy(i).start()
    small[1].start()

    @pl.loop(0, tiles)
    def _(i):
        c = order(i)
        tail_copy(0, c).start()
        tail_copy(1, c).start()

    small[2].start()
    small[3].start()

    @pl.loop(0, tiles)
    def _(c):
        head_copy(0, c).start()
        head_copy(1, c).start()
        q_copy(c).start()

    tap = lax.broadcasted_iota(jnp.int32, (half, LANES), 0)
    lane = lax.broadcasted_iota(jnp.int32, (half, LANES), 1)
    strip = lax.broadcasted_iota(jnp.int32, (16, LANES), 1) // members
    pick2 = [(strip % 2 == i).astype(BF16) for i in range(2)]
    pick4 = [(strip % 4 == i).astype(BF16) for i in range(4)]

    def short_masks(at, count):
        here = segc[pl.ds(at + block, count)]
        one[pl.ds(at, count)] = jnp.where(here == segc[pl.ds(at + block - 1, count)], 1.0, 0.0)
        two[pl.ds(at, count)] = jnp.where(here == segc[pl.ds(at + block - 2, count)], 1.0, 0.0)

    def feature(buf, x, lead, taps_rows, at, count):
        buf[pl.ds(lead, x.shape[0])] = x
        first = lead + x.shape[0] - count
        x0 = x[x.shape[0] - count:]
        x1, x2 = buf[pl.ds(first - 1, count)], buf[pl.ds(first - 2, count)]
        return (taps_rows[0:1] * x0 + (taps_rows[1:2] * x1) * one[pl.ds(at, count)]
                + (taps_rows[2:3] * x2) * two[pl.ds(at, count)])

    small[0].wait()
    for b in range(2):
        segc[pl.ds((b + 1) * block, block)] = column(seg[b:b + 1].astype(F32), block)
    short_masks(block, block)
    whole(raw, raw_sem.at[0]).wait()
    for i in range(3):
        edge_send[i, :, :width] = raw[i].astype(F32)[6:8].astype(BF16)
    edge_send[0, :, width:] = jnp.broadcast_to(seg[1:2].astype(F32), (2, block)).astype(BF16)
    for i in (1, 2):
        edge_send[i, :, width:] = jnp.zeros((2, block), BF16)

    def part(c, s):
        return pl.ds(pl.multiple_of(c * tile + s, LANES), LANES)

    def taps_of(i, at):
        return taps[i, :, at].astype(F32)

    small[1].wait()

    def produce(step):
        c = order(step)
        whole(kv.at[:, c, pl.ds(keep, rows - keep)], tail_sem.at[c]).wait()
        for s in range(0, tile, LANES):
            at, here = part(c, s), slice(s, s + LANES)
            feats = []
            for i in (1, 2):
                x = kv[i - 1, c, keep:, here].astype(F32)
                feats.append(feature(wide.at[i, s // LANES], x, 8, taps_of(i, at), block, block))
            pt[c, :, here] = (feats[0] * feats[1]).astype(BF16)

    def open_link():
        if not detours:
            pl.semaphore_wait(barrier, 1)
            edge_copy().start()
            return
        pl.semaphore_wait(barrier, jnp.where(turns | lands, 2, 1))
        edge_copy().start()

        @pl.when(lands)
        def _():
            pl.semaphore_signal(ready, inc=1, device_id={axis: 0}, device_id_type=pl.DeviceIdType.MESH)


    pl.when(has_right)(open_link)
    begin = 0
    for g in range(len(cuts) - 1):
        final = g == len(cuts) - 2
        end = tiles if final else cuts[g + 1] + 1
        pl.loop(begin, end)(produce)
        begin = end

        @pl.when(has_right)
        def _():
            if g == 0 and detours:
                @pl.when(turns)
                def _():
                    aside_copy(layer).start()
                    along_copy().start()

            if not (final and detours):
                part_copy(g).start()
                return

            @pl.when(turns)
            def _():
                part_copy(g, 1).start()

            @pl.when(jnp.logical_not(turns))
            def _():
                part_copy(g).start()

    small[2].wait()
    small[3].wait()
    wide_tap = lax.broadcasted_iota(jnp.int32, (block, block), 0)
    wide_lane = lax.broadcasted_iota(jnp.int32, (block, block), 1)
    turn = (wide_tap == lax.rem(block - wide_lane, block)).astype(BF16)
    turned = lax.dot_general(
        filters[...], turn, (((0,), (0,)), ((), ())), preferred_element_type=F32)
    hrev[...] = turned
    groups = turned.shape[0]
    glane = lax.broadcasted_iota(jnp.int32, turned.shape, 1)
    comb[...] = jnp.where((glane >= 1) & (glane <= half),
                          pltpu.roll(pltpu.roll(turned, half, 1), groups - 1, 0), turned)
    biasf[...] = bias[...].astype(F32)

    for b in range(4):
        own = segc[pl.ds(block + b * half, half)]
        start = own[0:1]
        own_head[pl.ds(b * half, half)] = jnp.where(own == start, 1.0, 0.0)
        row = seg[b // 2:b // 2 + 1].astype(F32)
        twin = pltpu.roll(jnp.broadcast_to(row, (8, block)), half, 1)[0:1]
        low = lane[0:1] < half
        row = jnp.where(low, row, twin) if b % 2 == 0 else jnp.where(low, twin, row)
        inner = jnp.where(lane < half, lane, lane - half)
        dmask[b] = jnp.where((own == row) & (inner <= tap), 1.0, 0.0).astype(BF16)

    def early_masks(b):
        start = segc[pl.ds(block + b * half, 8)][0:1]
        same = jnp.where(segc[pl.ds(b * half, block)] == start, 1.0, 0.0).astype(BF16)
        for i in range(2):
            emask[b, i] = same * jnp.concatenate([pick2[i]] * (block // 16), 0)

    early_masks(2)
    early_masks(3)
    later = (lane > tap).astype(BF16)

    @pl.when(has_left)
    def _():
        edge_copy().wait_recv()

    @pl.when(jnp.logical_not(has_left))
    def _():
        edge[...] = jnp.zeros_like(edge)

        @pl.loop(0, tiles)
        def _(c):
            halo[c] = jnp.zeros_like(halo[c])

    segc[pl.ds(0, block)] = column(edge[0, :, width:].astype(F32)[0:1], block)
    short_masks(0, block)
    early_masks(0)
    early_masks(1)

    quad = quads(half, members)

    @pl.loop(0, tiles)
    def _(c):
        if detours:
            @pl.when((me == 0) & (c == HANDOVER * tiles // 8))
            def _():
                pl.semaphore_wait(ready, detours)
                for z in reversed(range(detours)):
                    aside_copy(z).wait_recv()
                    onward_copy(z).start()

        whole(kv.at[:, c, pl.ds(0, keep)], head_sem.at[c]).wait()
        q_copy(c).wait()
        for s in range(0, tile, LANES):
            at, here, n = part(c, s), slice(s, s + LANES), s // LANES

            def feat(i, x):
                wide[i, n, pl.ds(6, 2)] = edge[i, :, at].astype(F32)
                return feature(wide.at[i, n], x.astype(F32), 8, taps_of(i, at), 0, x.shape[0])

            mid = (feat(1, kv[0, c, :block, here]) * feat(2, kv[1, c, :block, here])).astype(BF16)
            near = pt[c, :, here]
            first = (c * tile + s) // members

            def ring(source, g):
                base = jnp.broadcast_to(source[pl.ds(first + g, 1), :], (half, block))
                return pltpu.roll(base, 0, 1, stride=1, stride_axis=0).astype(BF16)

            for h in range(4):
                for i in range(2):
                    tables[c, n, h * half:(h + 1) * half, i * block:(i + 1) * block] = ring(hrev, 2 * h + i) * later
            own = [[ring(comb, 4 * h + 2 * i) for i in range(2)] for h in range(2)]
            blocks = (mid[:half], mid[half:], near[:half], near[half:])
            diag = []
            for b in range(4):
                left_side = jnp.concatenate([
                    jnp.concatenate([own[h][i] * dmask[b] for i in range(2)], 1) for h in range(2)], 0)
                right_side = jnp.concatenate([
                    blocks[b] * jnp.concatenate([pick4[i]] * (half // 16), 0) for i in range(4)], 0)
                every = jnp.dot(left_side, right_side, preferred_element_type=F32)
                diag.append(jnp.where(quad < 2, every[:half], every[half:]))
            brow = biasf[pl.ds((c * tile + s) // LANES, 1), :]
            fq = feat(0, qb[c, :, here])
            sure0 = jnp.concatenate(diag[:2], 0) + brow * mid.astype(F32)
            gate[c, n] = fq[:block] * own_head[pl.ds(0, block)]
            rest[c, n] = fq[:block] * sure0
            fresh = early(tables[c, n], mid, jnp.concatenate([mid[half:], near[:half]], 0), emask.at[2:4], quad)
            sure1 = jnp.concatenate(diag[2:], 0) + brow * near.astype(F32)
            out[block:, at] = (fq[block:] * (sure1 + fresh * own_head[pl.ds(block, block)])).astype(BF16)
            mids[c, :, here] = mid[:half]

    @pl.loop(0, tiles - last)
    def _(c):
        for g in range(len(cuts) - 2):
            @pl.when(has_left & (c == cuts[g]))
            def _():
                part_copy(g).wait_recv()

        for s in range(0, tile, LANES):
            out[:block, part(c, s)] = join(
                c, s // LANES, slice(s, s + LANES), halo, mids, tables, gate, rest, emask.at[0:2], quad)

    @pl.when(has_left)
    def _():
        part_copy(len(cuts) - 2).wait_recv()

    @pl.when(has_right)
    def _():
        edge_copy().wait_send()
        remote(pt, halo, send_sem.at[0], recv_sem.at[0]).wait_send()

    if detours:
        @pl.when(me == 0)
        def _():
            for z in range(detours):
                onward_copy(z).wait_send()


def finish(last, members, done, halo, mids, tables, gate, rest, emask, out, fresh, sem):
    rows, width = done.shape
    tiles, block, tile = halo.shape
    half = mids.shape[1]
    quad = quads(half, members)
    ready = width - last * tile
    copies = [
        pltpu.make_async_copy(done.at[at], out.at[at], sem.at[i])
        for i, at in enumerate((
            (pl.ds(0, block), pl.ds(0, ready)),
            (pl.ds(block, half), slice(None)),
            (pl.ds(block + half, half), slice(None))))]
    for copy in copies:
        copy.start()
    for i in range(last):
        c = tiles - last + i
        for s in range(0, tile, LANES):
            here = slice(s, s + LANES)
            fresh[i, :, here] = join(c, s // LANES, here, halo, mids, tables, gate, rest, emask.at[0:2], quad)
        copy = pltpu.make_async_copy(
            fresh.at[i], out.at[pl.ds(0, block), pl.ds(ready + i * tile, tile)], sem.at[3 + i])
        copy.start()
        copies.append(copy)
    for copy in copies:
        copy.wait()


def layers_of(mesh, axis):
    at = mesh.axis_names.index(axis)
    lines = np.moveaxis(mesh.devices, at, -1).reshape(-1, mesh.shape[axis])
    if lines.shape[1] % 4:
        return 1
    for line in lines:
        spots = [getattr(d, "coords", None) for d in line]
        if None in spots:
            return 1
        spots = np.array([tuple(spot) for spot in spots])
        spots = spots - spots[0]
        chip = np.arange(len(line)) // 2
        want = np.stack([np.zeros_like(chip), chip % 2, chip // 2], 1)
        if not np.array_equal(spots, want):
            return 1
    return lines.shape[1] // 4


def per_device(layers, queries, keys, values, segments, short_filters, mr_filter, mr_bias):
    rows, width = queries.shape
    block, groups = mr_filter.shape
    half = block // 2
    members = width // groups
    tile = min(TILE, width)
    tiles = width // tile
    parts = tile // LANES
    dma = pltpu.SemaphoreType.DMA
    chunked = lambda r: pltpu.VMEM((tiles, r, tile), BF16)
    last = min(LAST, tiles)
    detours = min(DETOURS, layers - 1) if tiles > 1 else 0
    vmem = pl.BlockSpec(memory_space=pltpu.VMEM)
    held = pl.pallas_call(
        functools.partial(kernel, "tok", members, tiles, last, detours),
        in_specs=[pl.BlockSpec(memory_space=pltpu.HBM)] * 7,
        out_specs=[vmem] * 7,
        out_shape=[
            pltpu.VMEM((rows, width), BF16),
            chunked(block),
            chunked(half),
            pltpu.VMEM((tiles, parts, 4 * half, 2 * block), BF16),
            pltpu.VMEM((tiles, parts, block, LANES), F32),
            pltpu.VMEM((tiles, parts, block, LANES), F32),
            pltpu.VMEM((4, 2, block, LANES), BF16),
        ],
        scratch_shapes=[
            pltpu.VMEM((rows // block, block), jnp.int32),
            pltpu.VMEM(short_filters.shape, BF16),
            pltpu.VMEM(mr_filter.shape, BF16),
            pltpu.VMEM((width // LANES, LANES), BF16),
            chunked(rows),
            pltpu.VMEM((2, tiles, rows, tile), BF16),
            chunked(block),
            pltpu.VMEM((3, 8, width), BF16),
            pltpu.VMEM((3, 2, width + block), BF16),
            pltpu.VMEM((3, 2, width + block), BF16),
            pltpu.VMEM((groups, block), F32),
            pltpu.VMEM((groups, block), F32),
            pltpu.VMEM((width // LANES, LANES), F32),
            pltpu.VMEM((block + rows, LANES), F32),
            pltpu.VMEM((rows, LANES), F32),
            pltpu.VMEM((rows, LANES), F32),
            pltpu.VMEM((rows, LANES), F32),
            pltpu.VMEM((4, half, LANES), BF16),
            pltpu.VMEM((3, parts, rows + 8, LANES), F32),
            dma((4,)), dma((1,)), dma((tiles,)), dma((tiles,)), dma((tiles,)),
            dma((1,)), dma((len(cuts_of(tiles, last)) - 1,)), dma((1,)), dma((1,)),
        ] + ([
            pltpu.VMEM((detours, block, tile // 4 * 3), BF16), dma((detours,)), dma((detours,)),
            pltpu.SemaphoreType.REGULAR,
        ] if detours else []),
        compiler_params=pltpu.CompilerParams(
            collective_id=0, has_side_effects=True, vmem_limit_bytes=24 * 2**20
        ),
    )(*(pltpu.with_memory_space_constraint(x, pltpu.HBM) for x in (
        queries, keys, values, segments.reshape(rows // block, block), short_filters,
        mr_filter, mr_bias.reshape(width // LANES, LANES))))
    return pl.pallas_call(
        functools.partial(finish, last, members),
        in_specs=[vmem] * 7,
        out_specs=pl.BlockSpec(memory_space=pltpu.HBM),
        out_shape=pltpu.HBM((rows, width), BF16),
        scratch_shapes=[pltpu.VMEM((last, block, tile), BF16), dma((3 + last,))],
        compiler_params=pltpu.CompilerParams(vmem_limit_bytes=8 * 2**20),
    )(*(pltpu.with_memory_space_constraint(x, pltpu.VMEM) for x in held))


def solution(mesh):
    placed = (
        P(("seq", "tok"), None),
        P(("seq", "tok"), None),
        P(("seq", "tok"), None),
        P(("seq", "tok")),
        P(),
        P(),
        P(),
    )
    return jax.shard_map(
        functools.partial(per_device, layers_of(mesh, "tok")), mesh=mesh, in_specs=placed, out_specs=P(("seq", "tok"), None), check_vma=False
    )
```

```python
import functools

import jax
import jax.numpy as jnp
import numpy as np
from jax import lax
from jax.experimental import pallas as pl
from jax.experimental.pallas import tpu as pltpu
from jax.sharding import PartitionSpec as P

LANES = 128
TILE = 512
LAST = 3
DETOURS = 3
HANDOVER = 5
F32, BF16 = jnp.float32, jnp.bfloat16


def column(row, block):
    return jnp.transpose(jnp.broadcast_to(row, (block, block)))


def cuts_of(tiles, last):
    inner = tiles - last
    return [0] + [n for n in (1,) if n < inner] + ([inner] if inner else []) + [tiles]


def quads(half, members):
    return lax.broadcasted_iota(jnp.int32, (half, LANES), 1) // (2 * members)


def early(table, low, high, masks, quad):
    half = quad.shape[0]
    right_side = jnp.concatenate([
        jnp.concatenate([x * masks[j, i] for j, x in enumerate((low, high))], 1)
        for i in range(2)], 0)
    every = jnp.dot(table, right_side, preferred_element_type=F32)
    picked = []
    for j in range(2):
        side = every[:, j * LANES:(j + 1) * LANES]
        parts = [side[h * half:(h + 1) * half] for h in range(4)]
        picked.append(jnp.where(quad == 0, parts[0], jnp.where(
            quad == 1, parts[1], jnp.where(quad == 2, parts[2], parts[3]))))
    return jnp.concatenate(picked, 0)


def join(c, n, here, halo, mids, tables, gate, rest, masks, quad):
    half = quad.shape[0]
    far = halo[c, :, here]
    fresh = early(tables[c, n], far, jnp.concatenate([far[half:], mids[c, :, here]], 0), masks, quad)
    return (gate[c, n] * fresh + rest[c, n]).astype(BF16)


def kernel(axis, members, tiles, last, detours, q, k, v, seg_hbm, taps_hbm, filters_hbm, bias_hbm,
           out, halo, mids, tables, gate, rest, emask,
           seg, taps, filters, bias, qb, kv, pt, raw, edge_send, edge,
           hrev, comb, biasf, segc, one, two, own_head, dmask, wide,
           small_sem, raw_sem, tail_sem, head_sem, q_sem,
           send_sem, recv_sem, small_send, small_recv, passing=None, pass_send=None, pass_recv=None, ready=None):
    rows, width = q.shape
    block = filters.shape[0]
    half = block // 2
    tile = width // tiles
    per = LANES // members
    keep = block - 16
    me = lax.axis_index(axis)
    size = lax.axis_size(axis)
    has_left, has_right = me > 0, me < size - 1
    left, right = jnp.maximum(me - 1, 0), jnp.minimum(me + 1, size - 1)
    turns = (me % 4 == 3) & (me // 4 < detours)
    layer = jnp.minimum(me // 4, max(detours - 1, 0))
    cuts = cuts_of(tiles, last)
    ends = [n + 1 for n in cuts[1:-1]] + [tiles]
    soon = min(2, tiles - 1)
    odd_one = cuts[-2]
    wide_part = tile // 4 * 3
    aside, along = pl.ds(0, wide_part), pl.ds(wide_part, tile - wide_part)
    barrier = pltpu.get_barrier_semaphore()

    def greet(device):
        pl.semaphore_signal(barrier, inc=1, device_id={axis: device}, device_id_type=pl.DeviceIdType.MESH)

    @pl.when(has_left)
    def _():
        greet(left)

    if detours:
        lands = (me % 4 == 0) & (me > 0) & (me // 4 <= detours)

        @pl.when(me == 0)
        def _():
            for z in range(detours):
                greet(4 * z + 3)
                greet(4 * z + 4)

    def cols(c):
        return pl.ds(pl.multiple_of(c * tile, tile), tile)

    def raw_copy(i):
        return pltpu.make_async_copy((q, k, v)[i].at[pl.ds(rows - 8, 8)], raw.at[i], raw_sem.at[0])

    def tail_copy(i, c, g):
        at = pl.ds(keep, rows - keep)
        return pltpu.make_async_copy((k, v)[i].at[at, cols(c)], kv.at[i, c, at], tail_sem.at[g])

    def head_copy(i, c):
        at = pl.ds(0, keep)
        return pltpu.make_async_copy((k, v)[i].at[at, cols(c)], kv.at[i, c, at], head_sem.at[jnp.where(c < soon, 0, 1)])

    def whole(ref, sem):
        return pltpu.make_async_copy(ref, ref, sem)

    def q_copy(c):
        return pltpu.make_async_copy(q.at[:, cols(c)], qb.at[c], q_sem.at[jnp.where(c < soon, 0, 1)])

    def remote(src, dst, s, r, device=right):
        return pltpu.make_async_remote_copy(
            src_ref=src, dst_ref=dst, send_sem=s, recv_sem=r,
            device_id={axis: device}, device_id_type=pl.DeviceIdType.MESH)

    def along_copy():
        return remote(pt.at[odd_one, :, along], halo.at[odd_one, :, along], send_sem.at[0], recv_sem.at[len(cuts) - 2])

    def aside_copy(z):
        return remote(pt.at[odd_one, :, aside], passing.at[z], send_sem.at[0], pass_recv.at[0], 0)

    def onward_copy(z):
        return remote(passing.at[z], halo.at[odd_one, :, aside], pass_send.at[0], recv_sem.at[len(cuts) - 2], 4 * z + 4)

    def order(i):
        return jnp.where(i == 0, odd_one, jnp.where(i <= odd_one, i - 1, i))

    def part_copy(g, skip=0):
        at = pl.ds(cuts[g] + skip, cuts[g + 1] - cuts[g] - skip)
        return remote(pt.at[at], halo.at[at], send_sem.at[0], recv_sem.at[g])

    def edge_copy():
        return remote(edge_send, edge, small_send.at[0], small_recv.at[0])

    small = [
        pltpu.make_async_copy(src, dst, small_sem.at[i])
        for i, (src, dst) in enumerate(
            ((seg_hbm, seg), (taps_hbm, taps), (filters_hbm, filters), (bias_hbm, bias)))
    ]
    small[0].start()
    for i in range(3):
        raw_copy(i).start()
    small[1].start()

    @pl.loop(0, tiles)
    def _(i):
        c = order(i)
        g = sum((i >= n).astype(jnp.int32) for n in ends[:-1])
        tail_copy(0, c, g).start()
        tail_copy(1, c, g).start()

    small[2].start()
    small[3].start()

    @pl.loop(0, tiles)
    def _(c):
        head_copy(0, c).start()
        head_copy(1, c).start()
        q_copy(c).start()

    tap = lax.broadcasted_iota(jnp.int32, (half, LANES), 0)
    lane = lax.broadcasted_iota(jnp.int32, (half, LANES), 1)
    strip = lax.broadcasted_iota(jnp.int32, (16, LANES), 1) // members
    pick2 = [(strip % 2 == i).astype(BF16) for i in range(2)]
    pick4 = [(strip % 4 == i).astype(BF16) for i in range(4)]

    def short_masks(at, count):
        here = segc[pl.ds(at + block, count)]
        one[pl.ds(at, count)] = jnp.where(here == segc[pl.ds(at + block - 1, count)], 1.0, 0.0)
        two[pl.ds(at, count)] = jnp.where(here == segc[pl.ds(at + block - 2, count)], 1.0, 0.0)

    def feature(buf, x, lead, taps_rows, at, count):
        buf[pl.ds(lead, x.shape[0])] = x
        first = lead + x.shape[0] - count
        x0 = x[x.shape[0] - count:]
        x1, x2 = buf[pl.ds(first - 1, count)], buf[pl.ds(first - 2, count)]
        return (taps_rows[0:1] * x0 + (taps_rows[1:2] * x1) * one[pl.ds(at, count)]
                + (taps_rows[2:3] * x2) * two[pl.ds(at, count)])

    small[0].wait()
    for b in range(2):
        segc[pl.ds((b + 1) * block, block)] = column(seg[b:b + 1].astype(F32), block)
    short_masks(block, block)
    whole(raw, raw_sem.at[0]).wait()
    for i in range(3):
        edge_send[i, :, :width] = raw[i].astype(F32)[6:8].astype(BF16)
    edge_send[0, :, width:] = jnp.broadcast_to(seg[1:2].astype(F32), (2, block)).astype(BF16)
    for i in (1, 2):
        edge_send[i, :, width:] = jnp.zeros((2, block), BF16)

    def part(c, s):
        return pl.ds(pl.multiple_of(c * tile + s, LANES), LANES)

    def taps_of(i, at):
        return taps[i, :, at].astype(F32)

    small[1].wait()

    def produce(step):
        c = order(step)
        for s in range(0, tile, LANES):
            at, here = part(c, s), slice(s, s + LANES)
            feats = []
            for i in (1, 2):
                x = kv[i - 1, c, keep:, here].astype(F32)
                feats.append(feature(wide.at[i, s // LANES], x, 8, taps_of(i, at), block, block))
            pt[c, :, here] = (feats[0] * feats[1]).astype(BF16)

    def open_link():
        if not detours:
            pl.semaphore_wait(barrier, 1)
            edge_copy().start()
            return
        pl.semaphore_wait(barrier, jnp.where(turns | lands, 2, 1))
        edge_copy().start()

        @pl.when(lands)
        def _():
            pl.semaphore_signal(ready, inc=1, device_id={axis: 0}, device_id_type=pl.DeviceIdType.MESH)


    pl.when(has_right)(open_link)
    begin = 0
    for g in range(len(cuts) - 1):
        final = g == len(cuts) - 2
        end = ends[g]
        whole(kv.at[:, pl.ds(begin, end - begin), pl.ds(keep, rows - keep)], tail_sem.at[g]).wait()
        pl.loop(begin, end)(produce)
        begin = end

        @pl.when(has_right)
        def _():
            if g == 0 and detours:
                @pl.when(turns)
                def _():
                    aside_copy(layer).start()
                    along_copy().start()

            if not (final and detours):
                part_copy(g).start()
                return

            @pl.when(turns)
            def _():
                part_copy(g, 1).start()

            @pl.when(jnp.logical_not(turns))
            def _():
                part_copy(g).start()

    small[2].wait()
    small[3].wait()
    wide_tap = lax.broadcasted_iota(jnp.int32, (block, block), 0)
    wide_lane = lax.broadcasted_iota(jnp.int32, (block, block), 1)
    turn = (wide_tap == lax.rem(block - wide_lane, block)).astype(BF16)
    turned = lax.dot_general(
        filters[...], turn, (((0,), (0,)), ((), ())), preferred_element_type=F32)
    hrev[...] = turned
    groups = turned.shape[0]
    glane = lax.broadcasted_iota(jnp.int32, turned.shape, 1)
    comb[...] = jnp.where((glane >= 1) & (glane <= half),
                          pltpu.roll(pltpu.roll(turned, half, 1), groups - 1, 0), turned)
    biasf[...] = bias[...].astype(F32)

    for b in range(4):
        own = segc[pl.ds(block + b * half, half)]
        start = own[0:1]
        own_head[pl.ds(b * half, half)] = jnp.where(own == start, 1.0, 0.0)
        row = seg[b // 2:b // 2 + 1].astype(F32)
        twin = pltpu.roll(jnp.broadcast_to(row, (8, block)), half, 1)[0:1]
        low = lane[0:1] < half
        row = jnp.where(low, row, twin) if b % 2 == 0 else jnp.where(low, twin, row)
        inner = jnp.where(lane < half, lane, lane - half)
        dmask[b] = jnp.where((own == row) & (inner <= tap), 1.0, 0.0).astype(BF16)

    def early_masks(b):
        start = segc[pl.ds(block + b * half, 8)][0:1]
        same = jnp.where(segc[pl.ds(b * half, block)] == start, 1.0, 0.0).astype(BF16)
        for i in range(2):
            emask[b, i] = same * jnp.concatenate([pick2[i]] * (block // 16), 0)

    early_masks(2)
    early_masks(3)
    later = (lane > tap).astype(BF16)

    @pl.when(has_left)
    def _():
        edge_copy().wait_recv()

    @pl.when(jnp.logical_not(has_left))
    def _():
        edge[...] = jnp.zeros_like(edge)

        @pl.loop(0, tiles)
        def _(c):
            halo[c] = jnp.zeros_like(halo[c])

    segc[pl.ds(0, block)] = column(edge[0, :, width:].astype(F32)[0:1], block)
    short_masks(0, block)
    early_masks(0)
    early_masks(1)

    quad = quads(half, members)

    @pl.loop(0, tiles)
    def _(c):
        if detours:
            @pl.when((me == 0) & (c == HANDOVER * tiles // 8))
            def _():
                pl.semaphore_wait(ready, detours)
                whole(passing, pass_recv.at[0]).wait()
                for z in reversed(range(detours)):
                    onward_copy(z).start()

        for g, (a, b) in enumerate(((0, soon), (soon, tiles))):
            @pl.when(c == a)
            def _():
                whole(kv.at[:, pl.ds(a, b - a), pl.ds(0, keep)], head_sem.at[g]).wait()
                whole(qb.at[pl.ds(a, b - a)], q_sem.at[g]).wait()

        for s in range(0, tile, LANES):
            at, here, n = part(c, s), slice(s, s + LANES), s // LANES

            def feat(i, x):
                wide[i, n, pl.ds(6, 2)] = edge[i, :, at].astype(F32)
                return feature(wide.at[i, n], x.astype(F32), 8, taps_of(i, at), 0, x.shape[0])

            mid = (feat(1, kv[0, c, :block, here]) * feat(2, kv[1, c, :block, here])).astype(BF16)
            near = pt[c, :, here]
            first = (c * tile + s) // members

            def ring(source, g):
                base = jnp.broadcast_to(source[pl.ds(first + g, 1), :], (half, block))
                return pltpu.roll(base, 0, 1, stride=1, stride_axis=0).astype(BF16)

            for h in range(4):
                for i in range(2):
                    tables[c, n, h * half:(h + 1) * half, i * block:(i + 1) * block] = ring(hrev, 2 * h + i) * later
            own = [[ring(comb, 4 * h + 2 * i) for i in range(2)] for h in range(2)]
            blocks = (mid[:half], mid[half:], near[:half], near[half:])
            diag = []
            for b in range(4):
                left_side = jnp.concatenate([
                    jnp.concatenate([own[h][i] * dmask[b] for i in range(2)], 1) for h in range(2)], 0)
                right_side = jnp.concatenate([
                    blocks[b] * jnp.concatenate([pick4[i]] * (half // 16), 0) for i in range(4)], 0)
                every = jnp.dot(left_side, right_side, preferred_element_type=F32)
                diag.append(jnp.where(quad < 2, every[:half], every[half:]))
            brow = biasf[pl.ds((c * tile + s) // LANES, 1), :]
            fq = feat(0, qb[c, :, here])
            sure0 = jnp.concatenate(diag[:2], 0) + brow * mid.astype(F32)
            gate[c, n] = fq[:block] * own_head[pl.ds(0, block)]
            rest[c, n] = fq[:block] * sure0
            fresh = early(tables[c, n], mid, jnp.concatenate([mid[half:], near[:half]], 0), emask.at[2:4], quad)
            sure1 = jnp.concatenate(diag[2:], 0) + brow * near.astype(F32)
            out[block:, at] = (fq[block:] * (sure1 + fresh * own_head[pl.ds(block, block)])).astype(BF16)
            mids[c, :, here] = mid[:half]

    @pl.loop(0, tiles - last)
    def _(c):
        for g in range(len(cuts) - 2):
            @pl.when(has_left & (c == cuts[g]))
            def _():
                part_copy(g).wait_recv()

        for s in range(0, tile, LANES):
            out[:block, part(c, s)] = join(
                c, s // LANES, slice(s, s + LANES), halo, mids, tables, gate, rest, emask.at[0:2], quad)

    @pl.when(has_left)
    def _():
        part_copy(len(cuts) - 2).wait_recv()

    @pl.when(has_right)
    def _():
        edge_copy().wait_send()
        remote(pt, halo, send_sem.at[0], recv_sem.at[0]).wait_send()

    if detours:
        @pl.when(me == 0)
        def _():
            whole(passing, pass_send.at[0]).wait()


def finish(last, members, done, halo, mids, tables, gate, rest, emask, out, fresh, sem):
    rows, width = done.shape
    tiles, block, tile = halo.shape
    half = mids.shape[1]
    quad = quads(half, members)
    ready = width - last * tile
    copies = [
        pltpu.make_async_copy(done.at[at], out.at[at], sem.at[i])
        for i, at in enumerate((
            (pl.ds(0, block), pl.ds(0, ready)),
            (pl.ds(block, half), slice(None)),
            (pl.ds(block + half, half), slice(None))))]
    for copy in copies:
        copy.start()
    for i in range(last):
        c = tiles - last + i
        for s in range(0, tile, LANES):
            here = slice(s, s + LANES)
            fresh[i, :, here] = join(c, s // LANES, here, halo, mids, tables, gate, rest, emask.at[0:2], quad)
        copy = pltpu.make_async_copy(
            fresh.at[i], out.at[pl.ds(0, block), pl.ds(ready + i * tile, tile)], sem.at[3 + i])
        copy.start()
        copies.append(copy)
    for copy in copies:
        copy.wait()


def layers_of(mesh, axis):
    at = mesh.axis_names.index(axis)
    lines = np.moveaxis(mesh.devices, at, -1).reshape(-1, mesh.shape[axis])
    if lines.shape[1] % 4:
        return 1
    for line in lines:
        spots = [getattr(d, "coords", None) for d in line]
        if None in spots:
            return 1
        spots = np.array([tuple(spot) for spot in spots])
        spots = spots - spots[0]
        chip = np.arange(len(line)) // 2
        want = np.stack([np.zeros_like(chip), chip % 2, chip // 2], 1)
        if not np.array_equal(spots, want):
            return 1
    return lines.shape[1] // 4


def per_device(layers, queries, keys, values, segments, short_filters, mr_filter, mr_bias):
    rows, width = queries.shape
    block, groups = mr_filter.shape
    half = block // 2
    members = width // groups
    tile = min(TILE, width)
    tiles = width // tile
    parts = tile // LANES
    dma = pltpu.SemaphoreType.DMA
    chunked = lambda r: pltpu.VMEM((tiles, r, tile), BF16)
    last = min(LAST, tiles)
    detours = min(DETOURS, layers - 1) if tiles > 1 else 0
    vmem = pl.BlockSpec(memory_space=pltpu.VMEM)
    held = pl.pallas_call(
        functools.partial(kernel, "tok", members, tiles, last, detours),
        in_specs=[pl.BlockSpec(memory_space=pltpu.HBM)] * 7,
        out_specs=[vmem] * 7,
        out_shape=[
            pltpu.VMEM((rows, width), BF16),
            chunked(block),
            chunked(half),
            pltpu.VMEM((tiles, parts, 4 * half, 2 * block), BF16),
            pltpu.VMEM((tiles, parts, block, LANES), F32),
            pltpu.VMEM((tiles, parts, block, LANES), F32),
            pltpu.VMEM((4, 2, block, LANES), BF16),
        ],
        scratch_shapes=[
            pltpu.VMEM((rows // block, block), jnp.int32),
            pltpu.VMEM(short_filters.shape, BF16),
            pltpu.VMEM(mr_filter.shape, BF16),
            pltpu.VMEM((width // LANES, LANES), BF16),
            chunked(rows),
            pltpu.VMEM((2, tiles, rows, tile), BF16),
            chunked(block),
            pltpu.VMEM((3, 8, width), BF16),
            pltpu.VMEM((3, 2, width + block), BF16),
            pltpu.VMEM((3, 2, width + block), BF16),
            pltpu.VMEM((groups, block), F32),
            pltpu.VMEM((groups, block), F32),
            pltpu.VMEM((width // LANES, LANES), F32),
            pltpu.VMEM((block + rows, LANES), F32),
            pltpu.VMEM((rows, LANES), F32),
            pltpu.VMEM((rows, LANES), F32),
            pltpu.VMEM((rows, LANES), F32),
            pltpu.VMEM((4, half, LANES), BF16),
            pltpu.VMEM((3, parts, rows + 8, LANES), F32),
            dma((4,)), dma((1,)), dma((len(cuts_of(tiles, last)) - 1,)), dma((2,)), dma((2,)),
            dma((1,)), dma((len(cuts_of(tiles, last)) - 1,)), dma((1,)), dma((1,)),
        ] + ([
            pltpu.VMEM((detours, block, tile // 4 * 3), BF16), dma((1,)), dma((1,)),
            pltpu.SemaphoreType.REGULAR,
        ] if detours else []),
        compiler_params=pltpu.CompilerParams(
            collective_id=0, has_side_effects=True, vmem_limit_bytes=24 * 2**20
        ),
    )(*(pltpu.with_memory_space_constraint(x, pltpu.HBM) for x in (
        queries, keys, values, segments.reshape(rows // block, block), short_filters,
        mr_filter, mr_bias.reshape(width // LANES, LANES))))
    return pl.pallas_call(
        functools.partial(finish, last, members),
        in_specs=[vmem] * 7,
        out_specs=pl.BlockSpec(memory_space=pltpu.HBM),
        out_shape=pltpu.HBM((rows, width), BF16),
        scratch_shapes=[pltpu.VMEM((last, block, tile), BF16), dma((3 + last,))],
        compiler_params=pltpu.CompilerParams(vmem_limit_bytes=8 * 2**20),
    )(*(pltpu.with_memory_space_constraint(x, pltpu.VMEM) for x in held))


def solution(mesh):
    placed = (
        P(("seq", "tok"), None),
        P(("seq", "tok"), None),
        P(("seq", "tok"), None),
        P(("seq", "tok")),
        P(),
        P(),
        P(),
    )
    return jax.shard_map(
        functools.partial(per_device, layers_of(mesh, "tok")), mesh=mesh, in_specs=placed, out_specs=P(("seq", "tok"), None), check_vma=False
    )
```

```python
import functools

import jax
import jax.numpy as jnp
import numpy as np
from jax import lax
from jax.experimental import pallas as pl
from jax.experimental.pallas import tpu as pltpu
from jax.sharding import PartitionSpec as P

LANES = 128
TILE = 512
LAST = 3
DETOURS = 3
HANDOVER = 5
F32, BF16 = jnp.float32, jnp.bfloat16


def column(row, block):
    return jnp.transpose(jnp.broadcast_to(row, (block, block)))


def cuts_of(tiles, last):
    inner = tiles - last
    return [0] + [n for n in (1,) if n < inner] + ([inner] if inner else []) + [tiles]


def quads(half, members):
    return lax.broadcasted_iota(jnp.int32, (half, LANES), 1) // (2 * members)


def early(table, low, high, masks, quad):
    half = quad.shape[0]
    right_side = jnp.concatenate([
        jnp.concatenate([x * masks[j, i] for j, x in enumerate((low, high))], 1)
        for i in range(2)], 0)
    every = jnp.dot(table, right_side, preferred_element_type=F32)
    picked = []
    for j in range(2):
        side = every[:, j * LANES:(j + 1) * LANES]
        parts = [side[h * half:(h + 1) * half] for h in range(4)]
        picked.append(jnp.where(quad == 0, parts[0], jnp.where(
            quad == 1, parts[1], jnp.where(quad == 2, parts[2], parts[3]))))
    return jnp.concatenate(picked, 0)


def join(c, n, here, halo, mids, tables, gate, rest, masks, quad):
    half = quad.shape[0]
    far = halo[c, :, here]
    fresh = early(tables[c, n], far, jnp.concatenate([far[half:], mids[c, :, here]], 0), masks, quad)
    return (gate[c, n] * fresh + rest[c, n]).astype(BF16)


def kernel(axis, members, tiles, last, detours, q, k, v, seg_hbm, taps_hbm, filters_hbm, bias_hbm,
           out, halo, mids, tables, gate, rest, emask,
           seg, taps, filters, bias, qb, kv, pt, raw, edge_send, edge,
           hrev, comb, biasf, segc, one, two, own_head, dmask, wide,
           small_sem, raw_sem, tail_sem, head_sem, q_sem,
           send_sem, recv_sem, small_send, small_recv, passing=None, pass_send=None, pass_recv=None, ready=None):
    rows, width = q.shape
    block = filters.shape[0]
    half = block // 2
    tile = width // tiles
    per = LANES // members
    keep = block - 16
    me = lax.axis_index(axis)
    size = lax.axis_size(axis)
    has_left, has_right = me > 0, me < size - 1
    left, right = jnp.maximum(me - 1, 0), jnp.minimum(me + 1, size - 1)
    turns = (me % 4 == 3) & (me // 4 < detours)
    layer = jnp.minimum(me // 4, max(detours - 1, 0))
    cuts = cuts_of(tiles, last)
    ends = [n + 1 for n in cuts[1:-1]] + [tiles]
    soon = min(2, tiles - 1)
    odd_one = cuts[-2]
    wide_part = tile // 4 * 3
    aside, along = pl.ds(0, wide_part), pl.ds(wide_part, tile - wide_part)
    barrier = pltpu.get_barrier_semaphore()

    def greet(device):
        pl.semaphore_signal(barrier, inc=1, device_id={axis: device}, device_id_type=pl.DeviceIdType.MESH)

    @pl.when(has_left)
    def _():
        greet(left)

    if detours:
        lands = (me % 4 == 0) & (me > 0) & (me // 4 <= detours)

        @pl.when(me == 0)
        def _():
            for z in range(detours):
                greet(4 * z + 3)
                greet(4 * z + 4)

    def cols(c):
        return pl.ds(pl.multiple_of(c * tile, tile), tile)

    def raw_copy(i):
        return pltpu.make_async_copy((q, k, v)[i].at[pl.ds(rows - 8, 8)], raw.at[i], raw_sem.at[0])

    def tail_copy(i, c, g):
        at = pl.ds(keep, rows - keep)
        return pltpu.make_async_copy((k, v)[i].at[at, cols(c)], kv.at[i, c, at], tail_sem.at[g])

    def head_copy(i, c):
        at = pl.ds(0, keep)
        return pltpu.make_async_copy((k, v)[i].at[at, cols(c)], kv.at[i, c, at], head_sem.at[jnp.where(c < soon, 0, 1)])

    def whole(ref, sem):
        return pltpu.make_async_copy(ref, ref, sem)

    def q_copy(c):
        return pltpu.make_async_copy(q.at[:, cols(c)], qb.at[c], q_sem.at[jnp.where(c < soon, 0, 1)])

    def remote(src, dst, s, r, device=right):
        return pltpu.make_async_remote_copy(
            src_ref=src, dst_ref=dst, send_sem=s, recv_sem=r,
            device_id={axis: device}, device_id_type=pl.DeviceIdType.MESH)

    def along_copy():
        return remote(pt.at[odd_one, :, along], halo.at[odd_one, :, along], send_sem.at[0], recv_sem.at[len(cuts) - 2])

    def aside_copy(z):
        return remote(pt.at[odd_one, :, aside], passing.at[z], send_sem.at[0], pass_recv.at[0], 0)

    def onward_copy(z):
        return remote(passing.at[z], halo.at[odd_one, :, aside], pass_send.at[0], recv_sem.at[len(cuts) - 2], 4 * z + 4)

    def order(i):
        return jnp.where(i == 0, odd_one, jnp.where(i <= odd_one, i - 1, i))

    def part_copy(g, skip=0):
        at = pl.ds(cuts[g] + skip, cuts[g + 1] - cuts[g] - skip)
        return remote(pt.at[at], halo.at[at], send_sem.at[0], recv_sem.at[g])

    def edge_copy():
        return remote(edge_send, edge, small_send.at[0], small_recv.at[0])

    small = [
        pltpu.make_async_copy(src, dst, small_sem.at[i])
        for i, (src, dst) in enumerate(
            ((seg_hbm, seg), (taps_hbm, taps), (filters_hbm, filters), (bias_hbm, bias)))
    ]
    small[0].start()
    for i in range(3):
        raw_copy(i).start()
    small[1].start()

    @pl.loop(0, tiles)
    def _(i):
        c = order(i)
        g = sum((i >= n).astype(jnp.int32) for n in ends[:-1])
        tail_copy(0, c, g).start()
        tail_copy(1, c, g).start()

    small[2].start()
    small[3].start()

    @pl.loop(0, tiles)
    def _(c):
        head_copy(0, c).start()
        head_copy(1, c).start()
        q_copy(c).start()

    tap = lax.broadcasted_iota(jnp.int32, (half, LANES), 0)
    lane = lax.broadcasted_iota(jnp.int32, (half, LANES), 1)
    strip = lax.broadcasted_iota(jnp.int32, (16, LANES), 1) // members
    pick2 = [(strip % 2 == i).astype(BF16) for i in range(2)]
    pick4 = [(strip % 4 == i).astype(BF16) for i in range(4)]

    def short_masks(at, count):
        here = segc[pl.ds(at + block, count)]
        one[pl.ds(at, count)] = jnp.where(here == segc[pl.ds(at + block - 1, count)], 1.0, 0.0)
        two[pl.ds(at, count)] = jnp.where(here == segc[pl.ds(at + block - 2, count)], 1.0, 0.0)

    def feature(buf, x, lead, taps_rows, at, count):
        buf[pl.ds(lead, x.shape[0])] = x
        first = lead + x.shape[0] - count
        x0 = x[x.shape[0] - count:]
        x1, x2 = buf[pl.ds(first - 1, count)], buf[pl.ds(first - 2, count)]
        return (taps_rows[0:1] * x0 + (taps_rows[1:2] * x1) * one[pl.ds(at, count)]
                + (taps_rows[2:3] * x2) * two[pl.ds(at, count)])

    small[0].wait()
    for b in range(2):
        segc[pl.ds((b + 1) * block, block)] = column(seg[b:b + 1].astype(F32), block)
    short_masks(block, block)
    whole(raw, raw_sem.at[0]).wait()
    for i in range(3):
        edge_send[i, :, :width] = raw[i].astype(F32)[6:8].astype(BF16)
    edge_send[0, :, width:] = jnp.broadcast_to(seg[1:2].astype(F32), (2, block)).astype(BF16)
    for i in (1, 2):
        edge_send[i, :, width:] = jnp.zeros((2, block), BF16)

    def part(c, s):
        return pl.ds(pl.multiple_of(c * tile + s, LANES), LANES)

    def taps_of(i, at):
        return taps[i, :, at].astype(F32)

    small[1].wait()

    def produce(step):
        c = order(step)
        for s in range(0, tile, LANES):
            at, here = part(c, s), slice(s, s + LANES)
            feats = []
            for i in (1, 2):
                x = kv[i - 1, c, keep:, here].astype(F32)
                feats.append(feature(wide.at[i, s // LANES], x, 8, taps_of(i, at), block, block))
            pt[c, :, here] = (feats[0] * feats[1]).astype(BF16)

    def open_link():
        if not detours:
            pl.semaphore_wait(barrier, 1)
            edge_copy().start()
            return
        pl.semaphore_wait(barrier, jnp.where(turns | lands, 2, 1))
        edge_copy().start()

        @pl.when(lands)
        def _():
            pl.semaphore_signal(ready, inc=1, device_id={axis: 0}, device_id_type=pl.DeviceIdType.MESH)


    pl.when(has_right)(open_link)
    begin = 0
    for g in range(len(cuts) - 1):
        final = g == len(cuts) - 2
        end = ends[g]
        whole(kv.at[:, pl.ds(begin, end - begin), pl.ds(keep, rows - keep)], tail_sem.at[g]).wait()
        pl.loop(begin, end)(produce)
        begin = end

        @pl.when(has_right)
        def _():
            if g == 0 and detours:
                @pl.when(turns)
                def _():
                    aside_copy(layer).start()
                    along_copy().start()

            if not (final and detours):
                part_copy(g).start()
                return

            @pl.when(turns)
            def _():
                part_copy(g, 1).start()

            @pl.when(jnp.logical_not(turns))
            def _():
                part_copy(g).start()

    small[2].wait()
    small[3].wait()
    wide_tap = lax.broadcasted_iota(jnp.int32, (block, block), 0)
    wide_lane = lax.broadcasted_iota(jnp.int32, (block, block), 1)
    turn = (wide_tap == lax.rem(block - wide_lane, block)).astype(BF16)
    turned = lax.dot_general(
        filters[...], turn, (((0,), (0,)), ((), ())), preferred_element_type=F32)
    hrev[...] = turned
    groups = turned.shape[0]
    glane = lax.broadcasted_iota(jnp.int32, turned.shape, 1)
    comb[...] = jnp.where((glane >= 1) & (glane <= half),
                          pltpu.roll(pltpu.roll(turned, half, 1), groups - 1, 0), turned)
    biasf[...] = bias[...].astype(F32)

    for b in range(4):
        own = segc[pl.ds(block + b * half, half)]
        start = own[0:1]
        own_head[pl.ds(b * half, half)] = jnp.where(own == start, 1.0, 0.0)
        row = seg[b // 2:b // 2 + 1].astype(F32)
        twin = pltpu.roll(jnp.broadcast_to(row, (8, block)), half, 1)[0:1]
        low = lane[0:1] < half
        row = jnp.where(low, row, twin) if b % 2 == 0 else jnp.where(low, twin, row)
        inner = jnp.where(lane < half, lane, lane - half)
        dmask[b] = jnp.where((own == row) & (inner <= tap), 1.0, 0.0).astype(BF16)

    def early_masks(b):
        start = segc[pl.ds(block + b * half, 8)][0:1]
        same = jnp.where(segc[pl.ds(b * half, block)] == start, 1.0, 0.0).astype(BF16)
        for i in range(2):
            emask[b, i] = same * jnp.concatenate([pick2[i]] * (block // 16), 0)

    early_masks(2)
    early_masks(3)
    later = (lane > tap).astype(BF16)

    @pl.when(has_left)
    def _():
        edge_copy().wait_recv()

    @pl.when(jnp.logical_not(has_left))
    def _():
        edge[...] = jnp.zeros_like(edge)

        @pl.loop(0, tiles)
        def _(c):
            halo[c] = jnp.zeros_like(halo[c])

    segc[pl.ds(0, block)] = column(edge[0, :, width:].astype(F32)[0:1], block)
    short_masks(0, block)
    early_masks(0)
    early_masks(1)

    quad = quads(half, members)

    @pl.loop(0, tiles)
    def _(c):
        if detours:
            @pl.when((me == 0) & (c == HANDOVER * tiles // 8))
            def _():
                pl.semaphore_wait(ready, detours)
                whole(passing, pass_recv.at[0]).wait()
                for z in reversed(range(detours)):
                    onward_copy(z).start()

        for g, (a, b) in enumerate(((0, soon), (soon, tiles))):
            @pl.when(c == a)
            def _():
                whole(kv.at[:, pl.ds(a, b - a), pl.ds(0, keep)], head_sem.at[g]).wait()
                whole(qb.at[pl.ds(a, b - a)], q_sem.at[g]).wait()

        for s in range(0, tile, LANES):
            at, here, n = part(c, s), slice(s, s + LANES), s // LANES

            def feat(i, x):
                wide[i, n, pl.ds(6, 2)] = edge[i, :, at].astype(F32)
                return feature(wide.at[i, n], x.astype(F32), 8, taps_of(i, at), 0, x.shape[0])

            mid = (feat(1, kv[0, c, :block, here]) * feat(2, kv[1, c, :block, here])).astype(BF16)
            near = pt[c, :, here]
            first = (c * tile + s) // members

            def ring(source, g):
                base = jnp.broadcast_to(source[pl.ds(first + g, 1), :], (half, block))
                return pltpu.roll(base, 0, 1, stride=1, stride_axis=0).astype(BF16)

            for h in range(4):
                for i in range(2):
                    tables[c, n, h * half:(h + 1) * half, i * block:(i + 1) * block] = ring(hrev, 2 * h + i) * later
            own = [[ring(comb, 4 * h + 2 * i) for i in range(2)] for h in range(2)]
            blocks = (mid[:half], mid[half:], near[:half], near[half:])
            diag = []
            for b in range(4):
                left_side = jnp.concatenate([
                    jnp.concatenate([own[h][i] * dmask[b] for i in range(2)], 1) for h in range(2)], 0)
                right_side = jnp.concatenate([
                    blocks[b] * jnp.concatenate([pick4[i]] * (half // 16), 0) for i in range(4)], 0)
                every = jnp.dot(left_side, right_side, preferred_element_type=F32)
                diag.append(jnp.where(quad < 2, every[:half], every[half:]))
            brow = biasf[pl.ds((c * tile + s) // LANES, 1), :]
            fq = feat(0, qb[c, :, here])
            sure0 = jnp.concatenate(diag[:2], 0) + brow * mid.astype(F32)
            gate[c, n] = fq[:block] * own_head[pl.ds(0, block)]
            rest[c, n] = fq[:block] * sure0
            fresh = early(tables[c, n], mid, jnp.concatenate([mid[half:], near[:half]], 0), emask.at[2:4], quad)
            sure1 = jnp.concatenate(diag[2:], 0) + brow * near.astype(F32)
            out[block:, at] = (fq[block:] * (sure1 + fresh * own_head[pl.ds(block, block)])).astype(BF16)
            mids[c, :, here] = mid[:half]

    @pl.loop(0, tiles - last)
    def _(c):
        for g in range(len(cuts) - 2):
            @pl.when(has_left & (c == cuts[g]))
            def _():
                part_copy(g).wait_recv()

        for s in range(0, tile, LANES):
            out[:block, part(c, s)] = join(
                c, s // LANES, slice(s, s + LANES), halo, mids, tables, gate, rest, emask.at[0:2], quad)

    @pl.when(has_left)
    def _():
        part_copy(len(cuts) - 2).wait_recv()

    @pl.when(has_right)
    def _():
        edge_copy().wait_send()
        remote(pt, halo, send_sem.at[0], recv_sem.at[0]).wait_send()

    if detours:
        @pl.when(me == 0)
        def _():
            whole(passing, pass_send.at[0]).wait()


def finish(last, members, done, halo, mids, tables, gate, rest, emask, out, fresh, sem):
    rows, width = done.shape
    tiles, block, tile = halo.shape
    half = mids.shape[1]
    quad = quads(half, members)
    ready = width - last * tile
    copies = [
        pltpu.make_async_copy(done.at[at], out.at[at], sem.at[0])
        for at in (
            (pl.ds(0, block), pl.ds(0, ready)),
            (pl.ds(block, rows - block), slice(None)))]
    for copy in copies:
        copy.start()
    for i in range(last):
        c = tiles - last + i
        for s in range(0, tile, LANES):
            here = slice(s, s + LANES)
            fresh[i, :, here] = join(c, s // LANES, here, halo, mids, tables, gate, rest, emask.at[0:2], quad)
        copy = pltpu.make_async_copy(
            fresh.at[i], out.at[pl.ds(0, block), pl.ds(ready + i * tile, tile)], sem.at[0])
        copy.start()
    pltpu.make_async_copy(done, out, sem.at[0]).wait()


def layers_of(mesh, axis):
    at = mesh.axis_names.index(axis)
    lines = np.moveaxis(mesh.devices, at, -1).reshape(-1, mesh.shape[axis])
    if lines.shape[1] % 4:
        return 1
    for line in lines:
        spots = [getattr(d, "coords", None) for d in line]
        if None in spots:
            return 1
        spots = np.array([tuple(spot) for spot in spots])
        spots = spots - spots[0]
        chip = np.arange(len(line)) // 2
        want = np.stack([np.zeros_like(chip), chip % 2, chip // 2], 1)
        if not np.array_equal(spots, want):
            return 1
    return lines.shape[1] // 4


def per_device(layers, queries, keys, values, segments, short_filters, mr_filter, mr_bias):
    rows, width = queries.shape
    block, groups = mr_filter.shape
    half = block // 2
    members = width // groups
    tile = min(TILE, width)
    tiles = width // tile
    parts = tile // LANES
    dma = pltpu.SemaphoreType.DMA
    chunked = lambda r: pltpu.VMEM((tiles, r, tile), BF16)
    last = min(LAST, tiles)
    detours = min(DETOURS, layers - 1) if tiles > 1 else 0
    vmem = pl.BlockSpec(memory_space=pltpu.VMEM)
    held = pl.pallas_call(
        functools.partial(kernel, "tok", members, tiles, last, detours),
        in_specs=[pl.BlockSpec(memory_space=pltpu.HBM)] * 7,
        out_specs=[vmem] * 7,
        out_shape=[
            pltpu.VMEM((rows, width), BF16),
            chunked(block),
            chunked(half),
            pltpu.VMEM((tiles, parts, 4 * half, 2 * block), BF16),
            pltpu.VMEM((tiles, parts, block, LANES), F32),
            pltpu.VMEM((tiles, parts, block, LANES), F32),
            pltpu.VMEM((4, 2, block, LANES), BF16),
        ],
        scratch_shapes=[
            pltpu.VMEM((rows // block, block), jnp.int32),
            pltpu.VMEM(short_filters.shape, BF16),
            pltpu.VMEM(mr_filter.shape, BF16),
            pltpu.VMEM((width // LANES, LANES), BF16),
            chunked(rows),
            pltpu.VMEM((2, tiles, rows, tile), BF16),
            chunked(block),
            pltpu.VMEM((3, 8, width), BF16),
            pltpu.VMEM((3, 2, width + block), BF16),
            pltpu.VMEM((3, 2, width + block), BF16),
            pltpu.VMEM((groups, block), F32),
            pltpu.VMEM((groups, block), F32),
            pltpu.VMEM((width // LANES, LANES), F32),
            pltpu.VMEM((block + rows, LANES), F32),
            pltpu.VMEM((rows, LANES), F32),
            pltpu.VMEM((rows, LANES), F32),
            pltpu.VMEM((rows, LANES), F32),
            pltpu.VMEM((4, half, LANES), BF16),
            pltpu.VMEM((3, parts, rows + 8, LANES), F32),
            dma((4,)), dma((1,)), dma((len(cuts_of(tiles, last)) - 1,)), dma((2,)), dma((2,)),
            dma((1,)), dma((len(cuts_of(tiles, last)) - 1,)), dma((1,)), dma((1,)),
        ] + ([
            pltpu.VMEM((detours, block, tile // 4 * 3), BF16), dma((1,)), dma((1,)),
            pltpu.SemaphoreType.REGULAR,
        ] if detours else []),
        compiler_params=pltpu.CompilerParams(
            collective_id=0, has_side_effects=True, vmem_limit_bytes=24 * 2**20
        ),
    )(*(pltpu.with_memory_space_constraint(x, pltpu.HBM) for x in (
        queries, keys, values, segments.reshape(rows // block, block), short_filters,
        mr_filter, mr_bias.reshape(width // LANES, LANES))))
    return pl.pallas_call(
        functools.partial(finish, last, members),
        in_specs=[vmem] * 7,
        out_specs=pl.BlockSpec(memory_space=pltpu.HBM),
        out_shape=pltpu.HBM((rows, width), BF16),
        scratch_shapes=[pltpu.VMEM((last, block, tile), BF16), dma((1,))],
        compiler_params=pltpu.CompilerParams(vmem_limit_bytes=8 * 2**20),
    )(*(pltpu.with_memory_space_constraint(x, pltpu.VMEM) for x in held))


def solution(mesh):
    placed = (
        P(("seq", "tok"), None),
        P(("seq", "tok"), None),
        P(("seq", "tok"), None),
        P(("seq", "tok")),
        P(),
        P(),
        P(),
    )
    return jax.shard_map(
        functools.partial(per_device, layers_of(mesh, "tok")), mesh=mesh, in_specs=placed, out_specs=P(("seq", "tok"), None), check_vma=False
    )
```
